128 devices in a mesh: row: 16 (over x, z_lo, core), col: 8 (over y, z_hi).
Axes of the slice: x: 4, y: 4, z: 4 (z_hi: 2, z_lo: 2; z = z_hi * 2 + z_lo), core: 2. Of those that a mesh axis runs over, the one named last changes fastest.
Arguments:
- phi: bfloat16 [80, 80, 80, 256], P('col', 'row'), may hold values from -1 to 1
- psi: bfloat16 [80, 80, 80, 256], P('col', 'row'), may hold values from -1 to 1
- points: int32 [16384], P(('row', 'col')), may hold values from 0 to 511999, as said below
Outputs:
- schur: float32 [16384, 16384], P('row', 'col')
- panel: float32 [16384, 256], P('row')
- potential: float32 [80, 80, 80, 256], P('col', 'row')
The draws below stay inside these ranges and needn't reach their ends.
Inputs may be any that keep to these rules, and one draw needn't show every extreme that they name: `points`: block k of 128 consecutive entries holds distinct indices (x 80 + y) * 80 + z of cells with x // 10 = k mod (8) and y // 5 = k div (8).
All inputs are finite; a program needn't handle non-finite values.
Results may differ from the reference program's by a relative error of at most 0.0003.
Values may be sent and summed in bfloat16 or wider, within the bound.
A program may use at most 128 MiB of HBM per device.

```python
import math
import jax
import jax.numpy as jnp
from jax import lax

NORB = 256
NMU = 16384
PB = 256
GX = 80
GY = 80
GZ = 80
CX = 10
CY = 5
MU_DEV = 128
N_ROW = 16


def draw_points(key, part):
    cells = CX * CY * GZ
    col_blocks = GX // CX

    def one_block(block_id):
        order = jax.random.permutation(jax.random.fold_in(key, block_id), cells)[:MU_DEV]
        row_blk = block_id // col_blocks
        col_blk = block_id % col_blocks
        local_x = order // (CY * GZ)
        local_y = order // GZ % CY
        local_z = order % GZ
        return ((col_blk * CX + local_x) * GY + row_blk * CY + local_y) * GZ + local_z
    blocks = jax.vmap(one_block)(jnp.arange(NMU // MU_DEV, dtype=jnp.int32))
    return blocks.reshape(NMU).astype(jnp.int32)


def wave_basis(length, weights):
    phases = jnp.arange(length, dtype=jnp.float32) * (2.0 * math.pi / length)
    waves = jnp.stack([jnp.ones_like(phases), jnp.cos(phases), jnp.sin(phases), jnp.cos(2.0 * phases), jnp.sin(2.0 * phases)])
    factors = jnp.array([1.0, 2.0, 2.0, 2.0, 2.0], jnp.float32) * weights
    return waves * jnp.sqrt(factors)[:, None]


def orbital_field(key):
    coeff_key, common_key, white_key = jax.random.split(key, 3)
    weights = jnp.array([0.3, 0.25, 0.25, 0.1, 0.1], jnp.float32)
    common_share = 0.3
    smooth_share = 0.5
    white_share = 1.0 - common_share - smooth_share
    basis_x = wave_basis(GX, weights)
    basis_y = wave_basis(GY, weights)
    basis_z = wave_basis(GZ, weights)
    coeffs = jax.random.normal(coeff_key, (5, 5, 5, NORB), jnp.float32)
    smooth = jnp.einsum('abco,cz->abzo', coeffs, basis_z)
    smooth = jnp.einsum('abzo,by->ayzo', smooth, basis_y)
    smooth = jnp.einsum('ayzo,ax->xyzo', smooth, basis_x)
    common = jax.random.normal(common_key, (NORB,), jnp.float32)
    white_part = jax.random.normal(white_key, (GX, GY, GZ, NORB), jnp.float32)
    orbital = math.sqrt(common_share) * common[None, None, None, :] + math.sqrt(smooth_share) * smooth + math.sqrt(white_share) * white_part
    return jnp.clip(0.25 * orbital, -1.0, 1.0).astype(jnp.bfloat16)


def draw_phi(key, part):
    return orbital_field(jax.random.fold_in(key, 101))


def draw_psi(key, part):
    return orbital_field(jax.random.fold_in(key, 202))


def setup_inputs(seed: int = 0) -> dict:
    splits = jax.random.split(jax.random.key(seed), 4)
    return {
        "phi": draw_phi(jax.random.fold_in(splits[3], 71), 0),
        "psi": draw_psi(jax.random.fold_in(splits[3], 71), 0),
        "points": draw_points(jax.random.fold_in(splits[3], 71), 0),
    }


shift_value = 4.0
box_length = 2.0

def signed_frequency(length):
    index = jnp.arange(length, dtype=jnp.int32)
    return jnp.where(2 * index < length, index, index - length).astype(jnp.float32)

def coulomb_table(x_freq, y_freq, z_freq):
    squared = x_freq[:, None, None] ** 2 + y_freq[None, :, None] ** 2 + z_freq[None, None, :] ** 2
    safe = jnp.maximum(squared, 1.0)
    return jnp.where(squared > 0.5, box_length * box_length / math.pi / safe, 0.0).astype(jnp.float32)

def reference(phi, psi, points):
    flat_phi = phi.reshape(GX * GY * GZ, NORB)
    flat_psi = psi.reshape(GX * GY * GZ, NORB)
    samples_a = jnp.take(flat_phi, points, axis=0)
    samples_b = jnp.take(flat_psi, points, axis=0)
    pivot_a = samples_a[:PB]
    pivot_b = samples_b[:PB]
    global_rows = jnp.arange(NMU, dtype=jnp.int32)
    pivots = jnp.arange(PB, dtype=jnp.int32)
    column_part = jnp.dot(samples_a.astype(jnp.float32), pivot_a.T.astype(jnp.float32), preferred_element_type=jnp.float32) * jnp.dot(samples_b.astype(jnp.float32), pivot_b.T.astype(jnp.float32), preferred_element_type=jnp.float32)
    column_part = column_part + shift_value * (global_rows[:, None] == pivots[None, :]).astype(jnp.float32)
    corner = column_part[:PB]
    lower_factor = jnp.linalg.cholesky(corner)
    inverse = lax.linalg.triangular_solve(lower_factor, jnp.eye(PB, dtype=jnp.float32), left_side=True, lower=True)
    panel = jnp.dot(column_part, inverse.T, precision=lax.Precision.HIGHEST)
    row_count = NMU // N_ROW

    def schur_rows(block_id):
        start = block_id * row_count
        rows_a = lax.dynamic_slice_in_dim(samples_a, start, row_count, 0)
        rows_b = lax.dynamic_slice_in_dim(samples_b, start, row_count, 0)
        rows_panel = lax.dynamic_slice_in_dim(panel, start, row_count, 0)
        index = start + jnp.arange(row_count, dtype=jnp.int32)
        gram = jnp.dot(rows_a.astype(jnp.float32), samples_a.T.astype(jnp.float32), preferred_element_type=jnp.float32) * jnp.dot(rows_b.astype(jnp.float32), samples_b.T.astype(jnp.float32), preferred_element_type=jnp.float32)
        gram = gram + shift_value * (index[:, None] == global_rows[None, :]).astype(jnp.float32)
        return gram - jnp.dot(rows_panel, panel.T, precision=lax.Precision.HIGHEST)
    schur = lax.map(schur_rows, jnp.arange(N_ROW, dtype=jnp.int32)).reshape(NMU, NMU)
    pair_rows = jnp.dot(flat_phi.astype(jnp.float32), pivot_a.T.astype(jnp.float32), preferred_element_type=jnp.float32) * jnp.dot(flat_psi.astype(jnp.float32), pivot_b.T.astype(jnp.float32), preferred_element_type=jnp.float32)
    fitting = jnp.dot(pair_rows, inverse.T, precision=lax.Precision.HIGHEST).reshape(GX, GY, GZ, PB)
    kernel = coulomb_table(signed_frequency(GX), signed_frequency(GY), signed_frequency(GZ))
    spectrum = jnp.fft.fftn(fitting, axes=(0, 1, 2))
    potential = jnp.real(jnp.fft.ifftn(spectrum * kernel[:, :, :, None], axes=(0, 1, 2)))
    return (schur, panel, potential.astype(jnp.float32))
```

```python
import functools
import math

import jax
import jax.numpy as jnp
import numpy as np
from jax import lax
from jax.experimental import pallas as pl
from jax.experimental.pallas import tpu as pltpu
from jax.sharding import PartitionSpec as P

NMU = 16384
PB = 256
N = 80
ROWS = 16
COLS = 8
CELLS = 4000
WIDE = 4096
CODE_LANE = 4000 - 31 * 128
LEVELS = 32766.0
LN2 = math.log(2.0)
shift_value = 4.0
highest = lax.Precision.HIGHEST
MESH = pl.DeviceIdType.MESH
VMEM = pl.BlockSpec(memory_space=pltpu.VMEM)
f32 = jnp.float32
bf16 = jnp.bfloat16


def hartley():
    angle = (np.outer(np.arange(N), np.arange(N)) % N) * (2.0 * np.pi / N)
    return np.cos(angle) + np.sin(angle)


def split_np(a):
    high = a.astype(np.float32).astype(jnp.bfloat16)
    low = (a - high.astype(np.float64)).astype(np.float32).astype(jnp.bfloat16)
    return high, low


def split(a):
    high = a.astype(bf16)
    return high, (a - high.astype(f32)).astype(bf16)


def mm(a, b):
    return jnp.dot(a, b, preferred_element_type=f32)


def mm_nt(a, b):
    return lax.dot_general(a, b, (((1,), (1,)), ((), ())), preferred_element_type=f32)


def scale_of(code):
    return jnp.exp(code.astype(f32) * (LN2 / 256.0))


def encode(peak):
    code = jnp.ceil(jnp.log(jnp.maximum(peak, 1e-30)) * (256.0 / LN2))
    return code, jnp.exp(code * (LN2 / 256.0))


def quantize(values, factor):
    q = jnp.clip(jnp.round(values * factor), -32767.0, 32767.0)
    return q.astype(jnp.int32).astype(jnp.int16)


def store_codes(out_ref, source_ref, peak):
    code, scale = encode(peak)
    factor = LEVELS / scale

    @pl.loop(0, 7)
    def _(j):
        at = pl.ds(pl.multiple_of(j * 512, 512), 512)
        out_ref[:, at] = quantize(source_ref[:, at], factor)

    out_ref[:, 3584:3968] = quantize(source_ref[:, 3584:3968], factor)
    last = jnp.clip(jnp.round(source_ref[:, 3968:4096] * factor), -32767.0, 32767.0)
    lane = lax.broadcasted_iota(jnp.int32, last.shape, 1)
    last = jnp.where(lane < CODE_LANE, last, jnp.where(lane == CODE_LANE, code, 0.0))
    out_ref[:, 3968:4096] = last.astype(jnp.int32).astype(jnp.int16)


def pivot_kernel(own_ref, out_ref, send1, recv1, send2, recv2, send3, recv3, local):
    r = lax.axis_index("row")
    c = lax.axis_index("col")
    barrier = pltpu.get_barrier_semaphore()
    for d in range(1, COLS):
        pl.semaphore_signal(
            barrier, inc=1, device_id={"row": r, "col": lax.rem(c + d, COLS)}, device_id_type=MESH
        )
    for d in range(1, ROWS):
        pl.semaphore_signal(
            barrier, inc=1, device_id={"row": lax.rem(r + d, ROWS), "col": c}, device_id_type=MESH
        )
    pl.semaphore_wait(barrier, COLS + ROWS - 2)

    def scatter(owner, j):
        return pltpu.make_async_remote_copy(
            own_ref.at[pl.ds(pl.multiple_of(j * 16, 16), 16)],
            out_ref.at[j, owner],
            send1.at[j],
            recv1.at[owner],
            device_id={"row": 0, "col": j},
            device_id_type=MESH,
        )

    for owner in range(2):

        @pl.when((r == 0) & (c == owner))
        def _():
            keep = pltpu.make_async_copy(
                own_ref.at[pl.ds(owner * 16, 16)], out_ref.at[owner, owner], local
            )
            keep.start()
            for d in range(1, COLS):
                scatter(owner, (owner + d) % COLS).start()
            keep.wait()

        @pl.when((r == 0) & (c != owner))
        def _():
            scatter(owner, c).wait_recv()

    def down(d):
        return pltpu.make_async_remote_copy(
            out_ref.at[c],
            out_ref.at[c],
            send2.at[d],
            recv2,
            device_id={"row": d, "col": c},
            device_id_type=MESH,
        )

    @pl.when(r == 0)
    def _():
        for d in range(1, ROWS):
            down(d).start()

    @pl.when(r != 0)
    def _():
        down(1).wait_recv()

    def across(d):
        return pltpu.make_async_remote_copy(
            out_ref.at[c],
            out_ref.at[c],
            send3.at[d],
            recv3.at[d],
            device_id={"row": r, "col": lax.rem(c + d, COLS)},
            device_id_type=MESH,
        )

    for d in range(1, COLS):
        across(d).start()
    for d in range(1, COLS):
        source = lax.rem(c + COLS - d, COLS)
        pltpu.make_async_remote_copy(
            out_ref.at[source],
            out_ref.at[source],
            send3.at[d],
            recv3.at[d],
            device_id={"row": r, "col": source},
            device_id_type=MESH,
        ).wait_recv()
    for d in range(1, COLS):
        across(d).wait_send()

    @pl.when(r == 0)
    def _():
        for d in range(1, ROWS):
            down(d).wait_send()

    for owner in range(2):

        @pl.when((r == 0) & (c == owner))
        def _():
            for d in range(1, COLS):
                scatter(owner, (owner + d) % COLS).wait_send()


def pivots_everywhere(own):
    dma = pltpu.SemaphoreType.DMA
    return pl.pallas_call(
        pivot_kernel,
        out_shape=jax.ShapeDtypeStruct((COLS, 2, 16, 2 * PB), bf16),
        in_specs=[VMEM],
        out_specs=VMEM,
        scratch_shapes=[
            dma((COLS,)),
            dma((2,)),
            dma((ROWS,)),
            dma,
            dma((COLS,)),
            dma((COLS,)),
            dma,
        ],
        compiler_params=pltpu.CompilerParams(collective_id=1, has_side_effects=True),
        name="pivots",
    )(own)


def pivot_halves(pivot_ref):
    rows = [pivot_ref[:, owner].reshape(128, 2 * PB) for owner in range(2)]
    both = jnp.concatenate(rows, axis=0)
    return both[:, :PB], both[:, PB:]


def cholesky_kernel(pivot_ref, inv_ref, w):
    pa, pb = pivot_halves(pivot_ref)
    i0 = lax.broadcasted_iota(jnp.int32, (PB, PB), 0)
    i1 = lax.broadcasted_iota(jnp.int32, (PB, PB), 1)
    eye = (i0 == i1).astype(f32)
    w[:, :PB] = mm_nt(pa, pa) * mm_nt(pb, pb) + shift_value * eye
    w[:, PB:] = eye
    nb = 32
    for block in range(PB // nb):
        g = block * nb
        panel = w[g : g + nb, :]
        sub = lax.broadcasted_iota(jnp.int32, (nb, 128), 0)
        for j in range(0, nb, 8):
            cols = [
                jnp.broadcast_to(panel[:, g + j + t : g + j + t + 1], (nb, 128)) for t in range(8)
            ]
            for t in range(8):
                k = j + t
                pivot = jnp.broadcast_to(cols[t][k : k + 1, :], (nb, 128))
                root = lax.rsqrt(pivot)
                root = root * (1.5 - 0.5 * pivot * root * root)
                left = cols[t] * root
                for u in range(t + 1, 8):
                    cols[u] = cols[u] - left * jnp.broadcast_to(
                        left[j + u : j + u + 1, :], (nb, 128)
                    )
                below = jnp.where(sub > k, left, 0.0)
                below = jnp.where(sub == k, 1.0 - root, below)
                wide = jnp.concatenate([below] * 4, axis=1)
                line = jnp.broadcast_to(panel[k : k + 1, :], (nb, 2 * PB))
                scaled = line * jnp.concatenate([root] * 4, axis=1)
                row_k = jnp.concatenate([sub == k] * 4, axis=1)
                panel = jnp.where(row_k, scaled, panel - wide * scaled)
        w[g : g + nb, :] = panel
        if g + nb < PB:
            left = panel[:, g + nb : PB] if (g + nb) % 128 == 0 else panel[:, :PB]
            if (g + nb) % 128 == 0:
                update = lax.dot_general(
                    left, panel, (((0,), (0,)), ((), ())), precision=highest, preferred_element_type=f32
                )
                w[g + nb :, :] = w[g + nb :, :] - update
            else:
                update = lax.dot_general(
                    left, panel, (((0,), (0,)), ((), ())), precision=highest, preferred_element_type=f32
                )
                w[g + nb :, :] = w[g + nb :, :] - update[g + nb :, :]
    inv_ref[...] = jnp.where(i0 >= i1, w[:, PB:], 0.0)


def inverse_factor(pivots):
    return pl.pallas_call(
        cholesky_kernel,
        out_shape=jax.ShapeDtypeStruct((PB, PB), f32),
        in_specs=[VMEM],
        out_specs=VMEM,
        scratch_shapes=[pltpu.VMEM((PB, 2 * PB), f32)],
        compiler_params=pltpu.CompilerParams(vmem_limit_bytes=20 << 20),
        name="cholesky",
    )(pivots)


def fitting_kernel(pivot_ref, inv_ref, phi_ref, psi_ref, out_ref, work, peak):
    pa, pb = pivot_halves(pivot_ref)
    inv = inv_ref[...]

    def chunk(at, width):
        pair = mm_nt(pa, phi_ref[at, :]) * mm_nt(pb, psi_ref[at, :])
        fit = jnp.dot(inv, pair, precision=highest, preferred_element_type=f32)
        work[:, at] = fit
        return fit

    peak[...] = jnp.zeros_like(peak)

    @pl.loop(0, 7)
    def _(j):
        fit = jnp.abs(chunk(pl.ds(pl.multiple_of(j * 512, 512), 512), 512))
        best = peak[...]
        for t in range(4):
            best = jnp.maximum(best, fit[:, t * 128 : t * 128 + 128])
        peak[...] = best

    fit = jnp.abs(chunk(slice(3584, 4000), 416))
    best = peak[...]
    for t in range(3):
        best = jnp.maximum(best, fit[:, t * 128 : t * 128 + 128])
    best = jnp.max(best, axis=1, keepdims=True)
    best = jnp.maximum(best, jnp.max(fit[:, 384:], axis=1, keepdims=True))
    store_codes(out_ref, work, best)


def fitting_codes(pivots, inverse, phi, psi):
    return pl.pallas_call(
        fitting_kernel,
        out_shape=jax.ShapeDtypeStruct((PB, WIDE), jnp.int16),
        in_specs=[VMEM] * 4,
        out_specs=VMEM,
        scratch_shapes=[pltpu.VMEM((PB, WIDE), f32), pltpu.VMEM((PB, 128), f32)],
        compiler_params=pltpu.CompilerParams(vmem_limit_bytes=30 << 20),
        name="fitting",
    )(pivots, inverse, phi, psi)


def conv_kernel(h_ref, wx_ref, wxt_ref, hy_ref, in_ref, out_ref, wz, planes, lines, flat, peak):
    wz[...] = jnp.zeros_like(wz)
    for part in range(2):
        h = h_ref[part]
        for n in range(4):
            wz[part, n, 32 * n : 32 * n + 80, 0:128] = h
            wz[part, n, 32 * n + 80 : 32 * n + 160, 128:256] = h
    scale = scale_of(in_ref[:, 3968:4096].astype(jnp.int32)[:, CODE_LANE : CODE_LANE + 1]) * (
        1.0 / LEVELS
    )

    def z_forward(start, n, line):
        q = in_ref[:, pl.ds(start, 256)].astype(jnp.int32).astype(f32)
        high, low = split(q)
        out = (mm(high, wz[0, n]) + mm(low, wz[0, n]) + mm(high, wz[1, n])) * scale
        planes[line] = out[:, :128]
        planes[line + 1] = out[:, 128:]

    @pl.loop(0, 6)
    def _(g):
        for n in range(4):
            z_forward(pl.multiple_of(g * 640 + n * 128, 128), n, g * 8 + n * 2)

    z_forward(3840, 0, 48)

    def lhs3(w_ref, rows, data):
        high, low = split(data)
        first = mm(w_ref[...], high)
        return first[:rows] + first[rows:] + mm(w_ref[:rows], low)

    @pl.loop(0, ROWS // 2)
    def _(pair):
        for yy in range(5):
            parts = []
            for s in range(2):
                at = pl.ds(pl.multiple_of((pair * 2 + s) * 16, 16), 16)
                parts.append(
                    jnp.concatenate([planes[x * 5 + yy, at, :] for x in range(10)], axis=0)
                )
            out = lhs3(wx_ref, 160, jnp.concatenate(parts, axis=1))
            for s in range(2):
                y = (pair * 2 + s) * 5 + yy
                lines[pl.ds(pl.multiple_of(y * 160, 160), 160), :] = out[:, s * 128 : s * 128 + 128]

    def signed(index):
        return jnp.where(2 * index < N, index, index - N).astype(f32)

    ky = signed(lax.broadcasted_iota(jnp.int32, (N, 128), 0))
    kz = signed(lax.broadcasted_iota(jnp.int32, (N, 128), 1))
    base = ky * ky + kz * kz

    @pl.loop(0, N)
    def _(kx):
        ats = [pl.ds(kx * 2 + s, N, stride=160) for s in range(2)]
        data = jnp.concatenate([lines[at, :] for at in ats], axis=1)
        fx = signed(jnp.full((N, 128), kx, jnp.int32))
        squared = base + fx * fx
        factor = (4.0 / math.pi / (N * N * N)) / jnp.maximum(squared, 1.0)
        factor = jnp.where(squared > 0.5, factor, 0.0)
        out = lhs3(hy_ref, N, data) * jnp.concatenate([factor, factor], axis=1)
        out = lhs3(hy_ref, N, out)
        for s in range(2):
            lines[ats[s], :] = out[:, s * 128 : s * 128 + 128]

    @pl.loop(0, ROWS // 2)
    def _(pair):
        for yy in range(5):
            parts = []
            for s in range(2):
                y = (pair * 2 + s) * 5 + yy
                parts.append(lines[pl.ds(pl.multiple_of(y * 160, 160), 160), :])
            out = lhs3(wxt_ref, 160, jnp.concatenate(parts, axis=1))
            for s in range(2):
                at = pl.ds(pl.multiple_of((pair * 2 + s) * 16, 16), 16)
                for x in range(10):
                    planes[x * 5 + yy, at, :] = out[x * 16 : x * 16 + 16, s * 128 : s * 128 + 128]

    def z_backward(n, line):
        high, low = split(jnp.concatenate([planes[line], planes[line + 1]], axis=1))
        return mm_nt(high, wz[0, n]) + mm_nt(low, wz[0, n]) + mm_nt(high, wz[1, n])

    peak[...] = jnp.zeros_like(peak)

    def keep(start, value):
        flat[:, pl.ds(start, 128)] = value
        peak[...] = jnp.maximum(peak[...], jnp.abs(value))

    @pl.loop(0, 6)
    def _(g):
        start = pl.multiple_of(g * 640, 128)
        before = None
        for n in range(4):
            out = z_backward(n, g * 8 + n * 2)
            first = out[:, :128]
            keep(start + n * 128, first if before is None else first + before)
            before = out[:, 128:]
        keep(start + 512, before)

    out = z_backward(0, 48)
    keep(3840, out[:, :128])
    keep(3968, out[:, 128:])
    store_codes(out_ref, flat, jnp.max(peak[...], axis=1, keepdims=True))


def convolve(codes):
    h = hartley()
    padded = np.zeros((N, 128))
    padded[:, :N] = h
    h_parts = np.stack(split_np(padded))
    wx = np.zeros((N, 2, 10, COLS, 2))
    for f in range(2):
        wx[:, f, :, :, f] = h.reshape(N, COLS, 10).transpose(0, 2, 1)
    wx = wx.reshape(160, 160)
    return pl.pallas_call(
        conv_kernel,
        out_shape=jax.ShapeDtypeStruct((PB, WIDE), jnp.int16),
        in_specs=[VMEM] * 5,
        out_specs=VMEM,
        scratch_shapes=[
            pltpu.VMEM((2, 4, 256, 256), bf16),
            pltpu.VMEM((50, 256, 128), f32),
            pltpu.VMEM((N * 160, 128), f32),
            pltpu.VMEM((PB, WIDE), f32),
            pltpu.VMEM((PB, 128), f32),
        ],
        compiler_params=pltpu.CompilerParams(vmem_limit_bytes=50 << 20),
        name="convolve",
    )(
        jnp.asarray(h_parts),
        jnp.asarray(np.concatenate(split_np(wx))),
        jnp.asarray(np.concatenate(split_np(wx.T))),
        jnp.asarray(np.concatenate(split_np(h))),
        codes,
    )


def decode_kernel(in_ref, out_ref):
    scale = scale_of(in_ref[:, 3968:4096].astype(jnp.int32)[:, CODE_LANE : CODE_LANE + 1]) * (
        1.0 / LEVELS
    )

    @pl.loop(0, 31)
    def _(j):
        at = pl.ds(pl.multiple_of(j * 128, 128), 128)
        block = in_ref[:, at].astype(jnp.int32).astype(f32) * scale
        out_ref[at, :] = block.T

    block = in_ref[:, 3968:4096].astype(jnp.int32).astype(f32) * scale
    out_ref[3968:4000, :] = block.T[:32]


def decode(codes):
    return pl.pallas_call(
        decode_kernel,
        out_shape=jax.ShapeDtypeStruct((CELLS, PB), f32),
        in_specs=[VMEM],
        out_specs=VMEM,
        compiler_params=pltpu.CompilerParams(vmem_limit_bytes=20 << 20),
        name="decode",
    )(codes)


def exchange(codes):
    return lax.all_to_all(codes, ("row", "col"), split_axis=0, concat_axis=0, tiled=True)


def hadamard_gram(left, right, left_index, right_index):
    first = mm_nt(left[:, :PB], right[:, :PB])
    second = mm_nt(left[:, PB:], right[:, PB:])
    return first * second + shift_value * (left_index[:, None] == right_index[None, :]).astype(f32)


def on_device(phi, psi, points):
    col_index = lax.axis_index("col")
    row_index = lax.axis_index("row")
    plane_count, line_count, depth_count, orbital_count = phi.shape
    flat_phi = phi.reshape(CELLS, orbital_count)
    flat_psi = psi.reshape(CELLS, orbital_count)
    global_x = points // (N * N)
    global_y = points // N % N
    global_z = points % N
    local_cell = (
        (global_x - col_index * plane_count) * line_count + global_y - row_index * line_count
    ) * N + global_z
    own = jnp.concatenate(
        [jnp.take(flat_phi, local_cell, axis=0), jnp.take(flat_psi, local_cell, axis=0)], axis=1
    )
    pivots = pivots_everywhere(own)
    row_samples = lax.all_gather(own, "col", axis=0, tiled=True)
    moves = []
    for block in range(ROWS * COLS):
        moves.append((block, (block % ROWS) * COLS + block // ROWS))
    col_samples = lax.all_gather(
        lax.ppermute(own, ("row", "col"), moves), "row", axis=0, tiled=True
    )
    inverse = inverse_factor(pivots)
    codes = fitting_codes(pivots, inverse, flat_phi, flat_psi)
    potential = decode(exchange(convolve(exchange(codes))))
    potential = potential.reshape(plane_count, line_count, depth_count, PB)

    pivot = pivots.transpose(1, 0, 2, 3).reshape(PB, 2 * PB)
    row_block = NMU // ROWS
    col_block = NMU // COLS
    row_global = row_index * row_block + jnp.arange(row_block, dtype=jnp.int32)
    col_global = col_index * col_block + jnp.arange(col_block, dtype=jnp.int32)
    ids = jnp.arange(PB, dtype=jnp.int32)
    panel_rows = jnp.dot(
        hadamard_gram(row_samples, pivot, row_global, ids), inverse.T, precision=highest
    )
    panel_cols = jnp.dot(
        hadamard_gram(col_samples, pivot, col_global, ids), inverse.T, precision=highest
    )
    schur = hadamard_gram(row_samples, col_samples, row_global, col_global) - jnp.dot(
        panel_rows, panel_cols.T, precision=lax.Precision.HIGH
    )
    return (schur, panel_rows, potential)


def solution(mesh):
    in_specs = (P("col", "row", None, None), P("col", "row", None, None), P(("row", "col")))
    out_specs = (P("row", "col"), P("row", None), P("col", "row", None, None))
    return jax.shard_map(
        on_device, mesh=mesh, in_specs=in_specs, out_specs=out_specs, check_vma=False
    )
```

```python
import functools
import math

import jax
import jax.numpy as jnp
import numpy as np
from jax import lax
from jax.experimental import pallas as pl
from jax.experimental.pallas import tpu as pltpu
from jax.sharding import PartitionSpec as P

NMU = 16384
PB = 256
N = 80
ROWS = 16
COLS = 8
CELLS = 4000
WIDE = 4096
DEVICES = 128
WORDS = DEVICES * 16
CODE_LANE = 4000 - 31 * 128
LEVELS = 32766.0
LN2 = math.log(2.0)
shift_value = 4.0
highest = lax.Precision.HIGHEST
MESH = pl.DeviceIdType.MESH
VMEM = pl.BlockSpec(memory_space=pltpu.VMEM)
f32 = jnp.float32
bf16 = jnp.bfloat16


def hartley():
    angle = (np.outer(np.arange(N), np.arange(N)) % N) * (2.0 * np.pi / N)
    return np.cos(angle) + np.sin(angle)


def split_np(a):
    high = a.astype(np.float32).astype(jnp.bfloat16)
    low = (a - high.astype(np.float64)).astype(np.float32).astype(jnp.bfloat16)
    return high, low


def split(a):
    high = a.astype(bf16)
    return high, (a - high.astype(f32)).astype(bf16)


def mm(a, b):
    return jnp.dot(a, b, preferred_element_type=f32)


def mm_nt(a, b):
    return lax.dot_general(a, b, (((1,), (1,)), ((), ())), preferred_element_type=f32)


def encode(peak):
    code = jnp.ceil(jnp.log(jnp.maximum(peak, 1e-30)) * (256.0 / LN2))
    return code, jnp.exp(code * (LN2 / 256.0))


def words_of(low, high):
    return (low & 0xFFFF) | (high << 16)


def low_of(words):
    return ((words << 16) >> 16).astype(f32)


def high_of(words):
    return (words >> 16).astype(f32)


def quantize(values, factor):
    return jnp.clip(jnp.round(values * factor), -32767.0, 32767.0)


def store_codes(out_ref, source_ref, first, peak):
    code, scale = encode(peak)
    factor = LEVELS / scale
    rows = slice(first, first + 128)

    def tile(j):
        return quantize(source_ref[rows, pl.ds(j * 128, 128)], factor)

    def store(j, high):
        words = words_of(tile(j).astype(jnp.int32), high.astype(jnp.int32))
        out_ref[pl.ds(j, 128, stride=16), :] = words

    @pl.loop(0, 5)
    def _(group):
        for t in range(3):
            j = pl.multiple_of(group * 3, 1) + t
            store(j, tile(j + 16))

    last = tile(31)
    lane = lax.broadcasted_iota(jnp.int32, last.shape, 1)
    store(15, jnp.where(lane < CODE_LANE, last, jnp.where(lane == CODE_LANE, code, 0.0)))


def load_scale(in_ref):
    last = high_of(in_ref[pl.ds(15, 128, stride=16), :])
    return jnp.exp(last[:, CODE_LANE : CODE_LANE + 1] * (LN2 / 256.0)) * (1.0 / LEVELS)


def pivot_halves(pivot_ref):
    rows = [pivot_ref[:, owner].reshape(128, 2 * PB) for owner in range(2)]
    both = jnp.concatenate(rows, axis=0)
    return both[:, :PB], both[:, PB:]


def invert_factor(pa, pb, inv_ref, w):
    i0 = lax.broadcasted_iota(jnp.int32, (PB, PB), 0)
    i1 = lax.broadcasted_iota(jnp.int32, (PB, PB), 1)
    eye = (i0 == i1).astype(f32)
    w[:, :PB] = mm_nt(pa, pa) * mm_nt(pb, pb) + shift_value * eye
    w[:, PB:] = eye
    nb = 32
    for block in range(PB // nb):
        g = block * nb
        panel = w[g : g + nb, :]
        sub = lax.broadcasted_iota(jnp.int32, (nb, 128), 0)
        for j in range(0, nb, 8):
            cols = [
                jnp.broadcast_to(panel[:, g + j + t : g + j + t + 1], (nb, 128)) for t in range(8)
            ]
            for t in range(8):
                k = j + t
                pivot = jnp.broadcast_to(cols[t][k : k + 1, :], (nb, 128))
                root = lax.rsqrt(pivot)
                root = root * (1.5 - 0.5 * pivot * root * root)
                left = cols[t] * root
                for u in range(t + 1, 8):
                    cols[u] = cols[u] - left * jnp.broadcast_to(
                        left[j + u : j + u + 1, :], (nb, 128)
                    )
                below = jnp.where(sub > k, left, 0.0)
                below = jnp.where(sub == k, 1.0 - root, below)
                wide = jnp.concatenate([below] * 4, axis=1)
                line = jnp.broadcast_to(panel[k : k + 1, :], (nb, 2 * PB))
                scaled = line * jnp.concatenate([root] * 4, axis=1)
                row_k = jnp.concatenate([sub == k] * 4, axis=1)
                panel = jnp.where(row_k, scaled, panel - wide * scaled)
        w[g : g + nb, :] = panel
        if g + nb < PB:
            left = panel[:, g + nb : PB] if (g + nb) % 128 == 0 else panel[:, :PB]
            if (g + nb) % 128 == 0:
                update = lax.dot_general(
                    left, panel, (((0,), (0,)), ((), ())), precision=highest, preferred_element_type=f32
                )
                w[g + nb :, :] = w[g + nb :, :] - update
            else:
                update = lax.dot_general(
                    left, panel, (((0,), (0,)), ((), ())), precision=highest, preferred_element_type=f32
                )
                w[g + nb :, :] = w[g + nb :, :] - update[g + nb :, :]
    inv_ref[...] = jnp.where(i0 >= i1, w[:, PB:], 0.0)


def fit(pa, pb, inv, phi, psi, out_ref, work, peak):
    def chunk(at):
        pair = mm_nt(pa, phi[at, :]) * mm_nt(pb, psi[at, :])
        fitted = jnp.dot(inv, pair, precision=highest, preferred_element_type=f32)
        work[:, at] = fitted
        return jnp.abs(fitted)

    peak[...] = jnp.zeros_like(peak)

    @pl.loop(0, 7)
    def _(j):
        fitted = chunk(pl.ds(pl.multiple_of(j * 512, 512), 512))
        best = peak[...]
        for t in range(4):
            best = jnp.maximum(best, fitted[:, t * 128 : t * 128 + 128])
        peak[...] = best

    fitted = chunk(slice(3584, 4000))
    best = peak[...]
    for t in range(3):
        best = jnp.maximum(best, fitted[:, t * 128 : t * 128 + 128])
    best = jnp.max(best, axis=1, keepdims=True)
    best = jnp.maximum(best, jnp.max(fitted[:, 384:], axis=1, keepdims=True))
    for f in range(2):
        store_codes(out_ref.at[f], work, f * 128, best[f * 128 : f * 128 + 128])


def head_kernel(
    own_ref, phi_ref, psi_ref,
    out_ref, pivot_ref, inv_ref, rows_ref, cols_ref,
    phi, psi, w, work, peak, send1, recv1, send2, recv2, send3, recv3,
    send_row, recv_row, send_move, recv_move, send_col, recv_col, send_core, recv_core, local,
):
    r = lax.axis_index("row")
    c = lax.axis_index("col")
    half = r // 2
    core = lax.rem(r, 2)
    goal_row = 8 * core + c
    goal_col = half
    stays = (goal_row == r) & (goal_col == c)
    source_row = 2 * c + r // 8
    source_col = lax.rem(r, 8)

    def at(row, col):
        return {"row": row, "col": col}

    def remote(source, target, send, recv, device):
        return pltpu.make_async_remote_copy(
            source, target, send, recv, device_id=device, device_id_type=MESH
        )

    loads = [
        pltpu.make_async_copy(phi_ref, phi, local.at[0]),
        pltpu.make_async_copy(psi_ref, psi, local.at[1]),
    ]
    for load in loads:
        load.start()

    barrier = pltpu.get_barrier_semaphore()
    for d in range(1, COLS):
        pl.semaphore_signal(
            barrier, inc=1, device_id=at(r, lax.rem(c + d, COLS)), device_id_type=MESH
        )
    for d in range(1, ROWS):
        pl.semaphore_signal(
            barrier, inc=1, device_id=at(lax.rem(r + d, ROWS), c), device_id_type=MESH
        )

    @pl.when(jnp.logical_not(stays))
    def _():
        for device in (at(goal_row, goal_col), at(source_row, source_col)):
            pl.semaphore_signal(barrier, inc=1, device_id=device, device_id_type=MESH)
        pl.semaphore_wait(barrier, COLS + ROWS)

    @pl.when(stays)
    def _():
        pl.semaphore_wait(barrier, COLS + ROWS - 2)

    def scatter(owner, j):
        return remote(
            own_ref.at[pl.ds(pl.multiple_of(j * 16, 16), 16)],
            pivot_ref.at[j, owner],
            send1.at[j],
            recv1.at[owner],
            at(0, j),
        )

    for owner in range(2):

        @pl.when((r == 0) & (c == owner))
        def _():
            keep = pltpu.make_async_copy(
                own_ref.at[pl.ds(owner * 16, 16)], pivot_ref.at[owner, owner], local.at[2]
            )
            keep.start()
            for d in range(1, COLS):
                scatter(owner, (owner + d) % COLS).start()
            keep.wait()

        @pl.when((r == 0) & (c != owner))
        def _():
            scatter(owner, c).wait_recv()

    def down(d):
        return remote(pivot_ref.at[c], pivot_ref.at[c], send2.at[d], recv2, at(d, c))

    @pl.when(r == 0)
    def _():
        for d in range(1, ROWS):
            down(d).start()

    @pl.when(r != 0)
    def _():
        down(1).wait_recv()

    def across(d):
        return remote(
            pivot_ref.at[c], pivot_ref.at[c], send3.at[d], recv3.at[d], at(r, lax.rem(c + d, COLS))
        )

    for d in range(1, COLS):
        across(d).start()
    for d in range(1, COLS):
        source = lax.rem(c + COLS - d, COLS)
        remote(
            pivot_ref.at[source], pivot_ref.at[source], send3.at[d], recv3.at[d], at(r, source)
        ).wait_recv()

    keep_rows = pltpu.make_async_copy(own_ref, rows_ref.at[c], local.at[3])
    keep_rows.start()
    move = remote(own_ref, cols_ref.at[goal_row], send_move, recv_move, at(goal_row, goal_col))
    keep_move = pltpu.make_async_copy(own_ref, cols_ref.at[goal_row], local.at[4])

    @pl.when(jnp.logical_not(stays))
    def _():
        move.start()

    @pl.when(stays)
    def _():
        keep_move.start()

    def row_send(d):
        return remote(
            own_ref, rows_ref.at[c], send_row.at[d], recv_row.at[d], at(r, lax.rem(c + d, COLS))
        )

    for d in range(1, COLS):
        row_send(d).start()

    pa, pb = pivot_halves(pivot_ref)
    invert_factor(pa, pb, inv_ref, w)

    @pl.when(jnp.logical_not(stays))
    def _():
        remote(
            own_ref, cols_ref.at[r], send_move, recv_move, at(source_row, source_col)
        ).wait_recv()

    @pl.when(stays)
    def _():
        keep_move.wait()

    def col_send(d):
        return remote(
            cols_ref.at[r],
            cols_ref.at[r],
            send_col.at[d],
            recv_col.at[d],
            at(lax.rem(half + d, COLS) * 2 + core, c),
        )

    for d in range(1, COLS):
        col_send(d).start()

    def core_send(d):
        block = lax.rem(half + COLS - d, COLS) * 2 + core
        return remote(
            cols_ref.at[block],
            cols_ref.at[block],
            send_core.at[d],
            recv_core.at[d],
            at(half * 2 + 1 - core, c),
        )

    core_send(0).start()
    for load in loads:
        load.wait()
    fit(pa, pb, inv_ref[...], phi, psi, out_ref, work, peak)

    for d in range(1, COLS):
        block = lax.rem(half + COLS - d, COLS) * 2 + core
        remote(
            cols_ref.at[block], cols_ref.at[block], send_col.at[d], recv_col.at[d], at(block, c)
        ).wait_recv()
        core_send(d).start()
    keep_rows.wait()
    for d in range(1, COLS):
        source = lax.rem(c + COLS - d, COLS)
        remote(
            own_ref, rows_ref.at[source], send_row.at[d], recv_row.at[d], at(r, source)
        ).wait_recv()
    for d in range(COLS):
        block = lax.rem(half + COLS - d, COLS) * 2 + 1 - core
        remote(
            cols_ref.at[block],
            cols_ref.at[block],
            send_core.at[d],
            recv_core.at[d],
            at(half * 2 + 1 - core, c),
        ).wait_recv()

    @pl.when(jnp.logical_not(stays))
    def _():
        move.wait_send()

    for d in range(1, COLS):
        across(d).wait_send()
        row_send(d).wait_send()
        col_send(d).wait_send()
    for d in range(COLS):
        core_send(d).wait_send()

    @pl.when(r == 0)
    def _():
        for d in range(1, ROWS):
            down(d).wait_send()

    for owner in range(2):

        @pl.when((r == 0) & (c == owner))
        def _():
            for d in range(1, COLS):
                scatter(owner, (owner + d) % COLS).wait_send()


def head(own, phi, psi):
    dma = pltpu.SemaphoreType.DMA
    anywhere = pl.BlockSpec(memory_space=pl.ANY)
    return pl.pallas_call(
        head_kernel,
        out_shape=(
            jax.ShapeDtypeStruct((2, WORDS, 128), jnp.int32),
            jax.ShapeDtypeStruct((COLS, 2, 16, 2 * PB), bf16),
            jax.ShapeDtypeStruct((PB, PB), f32),
            jax.ShapeDtypeStruct((COLS, 128, 2 * PB), bf16),
            jax.ShapeDtypeStruct((ROWS, 128, 2 * PB), bf16),
        ),
        in_specs=[VMEM, anywhere, anywhere],
        out_specs=(VMEM,) * 5,
        scratch_shapes=[
            pltpu.VMEM((CELLS, PB), bf16),
            pltpu.VMEM((CELLS, PB), bf16),
            pltpu.VMEM((PB, 2 * PB), f32),
            pltpu.VMEM((PB, WIDE), f32),
            pltpu.VMEM((PB, 128), f32),
            dma((COLS,)),
            dma((2,)),
            dma((ROWS,)),
            dma,
            dma((COLS,)),
            dma((COLS,)),
            dma((COLS,)),
            dma((COLS,)),
            dma,
            dma,
            dma((COLS,)),
            dma((COLS,)),
            dma((COLS,)),
            dma((COLS,)),
            dma((5,)),
        ],
        compiler_params=pltpu.CompilerParams(
            collective_id=1, has_side_effects=True, vmem_limit_bytes=60 << 20
        ),
        name="head",
    )(own, phi, psi)


def half_convolution(f, hx, hxt, hy, wz, wzt, got, sent, high, low, planes, lines, flat, peak):
    scale = load_scale(got)

    @pl.loop(0, 4)
    def _(group):
        for t in range(4):
            j = group * 4 + t
            words = got[pl.ds(j, 128, stride=16), :]
            for s, value in enumerate((low_of(words), high_of(words))):
                at = pl.ds(pl.multiple_of((j + 16 * s) * 128, 128), 128)
                high[:, at], low[:, at] = split(value)

    def z_forward(n, start, line):
        at = pl.ds(start, 256)
        first = high[:, at]
        out = mm(jnp.concatenate([first, low[:, at], first], axis=1), wz[n]) * scale
        planes[line] = out[:, :128]
        planes[line + 1] = out[:, 128:]

    @pl.loop(0, 6)
    def _(g):
        for n in range(4):
            z_forward(n, pl.multiple_of(g * 640 + n * 128, 128), g * 8 + n * 2)

    z_forward(0, 3840, 48)

    def mm3(w, data):
        first, second = split(data)
        return mm(w, jnp.concatenate([first, first, second], axis=0))

    def both(value):
        return value[:, :128], value[:, 128:]

    def line_at(y):
        return pl.ds(pl.multiple_of(y * N, 16), N)

    @pl.loop(0, ROWS // 2)
    def _(pair):
        for yy in range(5):
            halves = []
            for s in range(2):
                at = pl.ds(pl.multiple_of((pair * 2 + s) * 8, 8), 8)
                halves.append(
                    jnp.concatenate([planes[x * 5 + yy, at, :] for x in range(10)], axis=0)
                )
            out = both(mm3(hx, jnp.concatenate(halves, axis=1)))
            for s in range(2):
                lines[line_at((pair * 2 + s) * 5 + yy), :] = out[s]

    def signed(index):
        return jnp.where(2 * index < N, index, index - N).astype(f32)

    ky = signed(lax.broadcasted_iota(jnp.int32, (N, 128), 0))
    kz = signed(lax.broadcasted_iota(jnp.int32, (N, 128), 1))
    base = ky * ky + kz * kz

    @pl.loop(0, N // 8)
    def _(group):
        ats = [pl.ds(group * 8 + t, N, stride=N) for t in range(8)]
        datas = [lines[at, :] for at in ats]
        outs = []
        for t in range(0, 8, 2):
            factors = []
            for s in range(2):
                fx = signed(jnp.full((N, 128), group * 8 + t + s, jnp.int32))
                squared = base + fx * fx
                factor = (4.0 / math.pi / (N * N * N)) / jnp.maximum(squared, 1.0)
                factors.append(jnp.where(squared > 0.5, factor, 0.0))
            out = mm3(hy, jnp.concatenate(datas[t : t + 2], axis=1))
            outs.extend(both(mm3(hy, out * jnp.concatenate(factors, axis=1))))
        for at, out in zip(ats, outs, strict=True):
            lines[at, :] = out

    @pl.loop(0, ROWS // 2)
    def _(pair):
        for yy in range(5):
            halves = [lines[line_at((pair * 2 + s) * 5 + yy), :] for s in range(2)]
            out = both(mm3(hxt, jnp.concatenate(halves, axis=1)))
            for s in range(2):
                at = pl.ds(pl.multiple_of((pair * 2 + s) * 8, 8), 8)
                for x in range(10):
                    planes[x * 5 + yy, at, :] = out[s][x * 8 : x * 8 + 8]

    def z_backward(n, line):
        first = split(planes[line])
        second = split(planes[line + 1])
        data = jnp.concatenate(
            [first[0], second[0], first[1], second[1], first[0], second[0]], axis=1
        )
        return both(mm_nt(data, wzt[n]))

    peak[...] = jnp.zeros_like(peak)

    @pl.loop(0, 6)
    def _(g):
        start = pl.multiple_of(g * 640, 128)
        best = peak[...]
        before = None
        for n in range(5):
            value = before
            if n < 4:
                out, after = z_backward(n, g * 8 + n * 2)
                value = out if before is None else out + before
                before = after
            flat[:, pl.ds(start + n * 128, 128)] = value
            best = jnp.maximum(best, jnp.abs(value))
        peak[...] = best

    best = peak[...]
    for t, value in enumerate(z_backward(0, 48)):
        flat[:, 3840 + t * 128 : 3968 + t * 128] = value
        best = jnp.maximum(best, jnp.abs(value))
    store_codes(sent, flat, 0, jnp.max(best, axis=1, keepdims=True))


def grams(left, right):
    return mm_nt(left[:, :PB], right[:, :PB]) * mm_nt(left[:, PB:], right[:, PB:])


def schur_tiles(pivot_ref, inv_ref, rows_ref, cols_ref, schur_ref, panel_ref, left3, right3, tiles, out_sem, r, c):
    pa, pb = pivot_halves(pivot_ref)
    pivots = jnp.concatenate([pa, pb], axis=1)
    inv = inv_ref[...]

    def shifted(gram, row, column):
        i = row + lax.broadcasted_iota(jnp.int32, gram.shape, 0)
        j = column + lax.broadcasted_iota(jnp.int32, gram.shape, 1)
        return gram + jnp.where(i == j, shift_value, 0.0)

    def panel_of(samples, row):
        return lax.dot_general(
            shifted(grams(samples, pivots), row, 0), inv, (((1,), (1,)), ((), ())),
            precision=highest, preferred_element_type=f32,
        )

    @pl.loop(0, 4)
    def _(i):
        at = pl.ds(pl.multiple_of(i * 256, 256), 256)
        panel = panel_of(rows_ref[at, :], r * 1024 + i * 256)
        panel_ref[at, :] = panel
        high, low = split(panel)
        left3[at, :] = jnp.concatenate([high, low, high], axis=1)

    @pl.loop(0, 8)
    def _(i):
        at = pl.ds(pl.multiple_of(i * 256, 256), 256)
        high, low = split(panel_of(cols_ref[at, :], c * 2048 + i * 256))
        right3[at, :] = jnp.concatenate([high, high, low], axis=1)

    def put(i, slot):
        return pltpu.make_async_copy(
            tiles.at[slot], schur_ref.at[pl.ds(pl.multiple_of(i * 128, 128), 128)], out_sem.at[slot]
        )

    @pl.loop(0, 4)
    def _(pair):
        for slot in range(2):
            i = pair * 2 + slot

            @pl.when(pair > 0)
            def _():
                put(i - 2, slot).wait()

            at = pl.ds(pl.multiple_of(i * 128, 128), 128)
            rows = rows_ref[at, :]
            left = left3[at, :]
            for j in range(4):
                cols = slice(j * 512, j * 512 + 512)
                gram = shifted(
                    grams(rows, cols_ref[cols, :]), r * 1024 + i * 128, c * 2048 + j * 512
                )
                tiles[slot, :, cols] = gram - mm_nt(left, right3[cols, :])
            put(i, slot).start()

    for slot in range(2):
        put(6 + slot, slot).wait()


def middle_kernel(
    h_ref, hx_ref, hxt_ref, hy_ref, codes_ref, pivot_ref, inv_ref, rows_ref, cols_ref,
    back_ref, panel_ref, schur_ref,
    got, sent, wz, wzt, high, low, planes, lines, flat, peak, left3, right3, tiles,
    send_there, recv_there, send_back, recv_back, own_sem, out_sem,
):
    r = lax.axis_index("row")
    c = lax.axis_index("col")
    me = r * COLS + c

    def at(i):
        device = lax.rem(me + i, DEVICES)
        return device, {"row": device // COLS, "col": lax.rem(device, COLS)}

    def block(i):
        return pl.ds(pl.multiple_of(i * 16, 16), 16)

    barrier = pltpu.get_barrier_semaphore()

    @pl.loop(1, DEVICES)
    def _(i):
        pl.semaphore_signal(barrier, inc=1, device_id=at(i)[1], device_id_type=MESH)

    pl.semaphore_wait(barrier, DEVICES - 1)

    def send_all(source, target, send, recv, keep):
        pltpu.make_async_copy(source.at[block(me)], target.at[block(me)], keep).start()

        @pl.loop(1, DEVICES)
        def _(i):
            device, where = at(i)
            pltpu.make_async_remote_copy(
                source.at[block(device)],
                target.at[block(me)],
                send,
                recv,
                device_id=where,
                device_id_type=MESH,
            ).start()

    def wait_all(ref, sem):
        most = ref.at[pl.ds(0, WORDS - 16)]
        pltpu.make_async_copy(most, most, sem).wait()

    def wait_own(source, target, keep):
        pltpu.make_async_copy(source.at[block(me)], target.at[block(me)], keep).wait()

    for f in range(2):
        send_all(codes_ref.at[f], got.at[f], send_there.at[f], recv_there.at[f], own_sem.at[f])

    wz[...] = jnp.zeros_like(wz)
    wzt[...] = jnp.zeros_like(wzt)
    for part, which in enumerate((0, 0, 1)):
        h = h_ref[which]
        for n in range(4):
            for s in range(2):
                first = 32 * n + 80 * s
                wz[n, part * 256 + first : part * 256 + first + 80, 128 * s : 128 * s + 128] = h
                lane = part * 256 + 128 * s
                wzt[n, first : first + 80, lane : lane + 128] = h

    schur_tiles(
        pivot_ref, inv_ref, rows_ref, cols_ref, schur_ref, panel_ref, left3, right3, tiles, out_sem, r, c
    )
    matrices = (hx_ref[...], hxt_ref[...], hy_ref[...])
    for f in range(2):
        wait_own(codes_ref.at[f], got.at[f], own_sem.at[f])
        wait_all(got.at[f], recv_there.at[f])
        half_convolution(
            f, *matrices, wz, wzt, got.at[f], sent.at[f], high, low, planes, lines, flat, peak
        )
        send_all(sent.at[f], back_ref.at[f], send_back.at[f], recv_back.at[f], own_sem.at[2 + f])
    for f in range(2):
        wait_own(sent.at[f], back_ref.at[f], own_sem.at[2 + f])
        wait_all(back_ref.at[f], recv_back.at[f])
    for f in range(2):
        wait_all(codes_ref.at[f], send_there.at[f])
        wait_all(sent.at[f], send_back.at[f])


def side_by_side(a):
    high, low = split_np(a)
    return jnp.asarray(np.concatenate([high, low, high], axis=1))


def middle(codes, pivots, inverse, rows, cols):
    h = hartley()
    padded = np.zeros((N, 128))
    padded[:, :N] = h
    h_parts = np.stack(split_np(padded))
    hx = h.reshape(N, COLS, 10).transpose(0, 2, 1).reshape(N, N)
    dma = pltpu.SemaphoreType.DMA
    return pl.pallas_call(
        middle_kernel,
        out_shape=(
            jax.ShapeDtypeStruct((2, WORDS, 128), jnp.int32),
            jax.ShapeDtypeStruct((NMU // ROWS, PB), f32),
            jax.ShapeDtypeStruct((NMU // ROWS, NMU // COLS), f32),
        ),
        in_specs=[VMEM] * 9,
        out_specs=(VMEM, VMEM, pl.BlockSpec(memory_space=pl.ANY)),
        scratch_shapes=[
            pltpu.VMEM((2, WORDS, 128), jnp.int32),
            pltpu.VMEM((2, WORDS, 128), jnp.int32),
            pltpu.VMEM((4, 768, 256), bf16),
            pltpu.VMEM((4, 256, 768), bf16),
            pltpu.VMEM((128, WIDE), bf16),
            pltpu.VMEM((128, WIDE), bf16),
            pltpu.VMEM((50, 128, 128), f32),
            pltpu.VMEM((N * N, 128), f32),
            pltpu.VMEM((128, WIDE), f32),
            pltpu.VMEM((128, 128), f32),
            pltpu.VMEM((NMU // ROWS, 768), bf16),
            pltpu.VMEM((NMU // COLS, 768), bf16),
            pltpu.VMEM((2, 128, NMU // COLS), f32),
            dma((2,)),
            dma((2,)),
            dma((2,)),
            dma((2,)),
            dma((4,)),
            dma((2,)),
        ],
        compiler_params=pltpu.CompilerParams(
            collective_id=2, has_side_effects=True, vmem_limit_bytes=60 << 20
        ),
        name="middle",
    )(
        jnp.asarray(h_parts),
        side_by_side(hx),
        side_by_side(hx.T),
        side_by_side(h),
        codes,
        pivots,
        inverse,
        rows,
        cols,
    )


def decode_kernel(in_ref, out_ref):
    for f in range(2):
        words_ref = in_ref.at[f]
        scale = load_scale(words_ref)
        lanes = slice(f * 128, f * 128 + 128)

        def put(tile, value):
            block = (value * scale).T
            at = pl.ds(pl.multiple_of(tile * 128, 128), 128)
            out_ref[at, lanes] = block

        @pl.loop(0, 5)
        def _(group):
            for t in range(3):
                words = words_ref[pl.ds(group * 3 + t, 128, stride=16), :]
                put(group * 3 + t, low_of(words))
                put(group * 3 + t + 16, high_of(words))

        words = words_ref[pl.ds(15, 128, stride=16), :]
        put(15, low_of(words))
        out_ref[3968:4000, lanes] = (high_of(words) * scale).T[:32]


def decode(codes):
    return pl.pallas_call(
        decode_kernel,
        out_shape=jax.ShapeDtypeStruct((CELLS, PB), f32),
        in_specs=[VMEM],
        out_specs=VMEM,
        compiler_params=pltpu.CompilerParams(vmem_limit_bytes=20 << 20),
        name="decode",
    )(codes)


def on_device(phi, psi, points):
    col_index = lax.axis_index("col")
    row_index = lax.axis_index("row")
    plane_count, line_count, depth_count, orbital_count = phi.shape
    flat_phi = phi.reshape(CELLS, orbital_count)
    flat_psi = psi.reshape(CELLS, orbital_count)
    global_x = points // (N * N)
    global_y = points // N % N
    global_z = points % N
    local_cell = (
        (global_x - col_index * plane_count) * line_count + global_y - row_index * line_count
    ) * N + global_z
    own = jnp.concatenate(
        [jnp.take(flat_phi, local_cell, axis=0), jnp.take(flat_psi, local_cell, axis=0)], axis=1
    )
    codes, pivots, inverse, row_samples, col_samples = head(own, flat_phi, flat_psi)
    row_samples = row_samples.reshape(NMU // ROWS, 2 * PB)
    col_samples = col_samples.reshape(NMU // COLS, 2 * PB)
    back, panel, schur = middle(codes, pivots, inverse, row_samples, col_samples)
    potential = decode(back).reshape(plane_count, line_count, depth_count, PB)
    return (schur, panel, potential)


def solution(mesh):
    in_specs = (P("col", "row", None, None), P("col", "row", None, None), P(("row", "col")))
    out_specs = (P("row", "col"), P("row", None), P("col", "row", None, None))
    return jax.shard_map(
        on_device, mesh=mesh, in_specs=in_specs, out_specs=out_specs, check_vma=False
    )
```

```python
import functools
import math

import jax
import jax.numpy as jnp
import numpy as np
from jax import lax
from jax.experimental import pallas as pl
from jax.experimental.pallas import tpu as pltpu
from jax.sharding import PartitionSpec as P

NMU = 16384
PB = 256
N = 80
ROWS = 16
COLS = 8
CELLS = 4000
WIDE = 4096
DEVICES = 128
WORDS = DEVICES * 16
CODE_LANE = 4000 - 31 * 128
LEVELS = 32766.0
LN2 = math.log(2.0)
shift_value = 4.0
highest = lax.Precision.HIGHEST
MESH = pl.DeviceIdType.MESH
VMEM = pl.BlockSpec(memory_space=pltpu.VMEM)
f32 = jnp.float32
bf16 = jnp.bfloat16


def hartley():
    angle = (np.outer(np.arange(N), np.arange(N)) % N) * (2.0 * np.pi / N)
    return np.cos(angle) + np.sin(angle)


def split_np(a):
    high = a.astype(np.float32).astype(jnp.bfloat16)
    low = (a - high.astype(np.float64)).astype(np.float32).astype(jnp.bfloat16)
    return high, low


def split(a):
    high = a.astype(bf16)
    return high, (a - high.astype(f32)).astype(bf16)


def mm(a, b):
    return jnp.dot(a, b, preferred_element_type=f32)


def mm_nt(a, b):
    return lax.dot_general(a, b, (((1,), (1,)), ((), ())), preferred_element_type=f32)


def encode(peak):
    code = jnp.ceil(jnp.log(jnp.maximum(peak, 1e-30)) * (256.0 / LN2))
    return code, jnp.exp(code * (LN2 / 256.0))


def words_of(low, high):
    return (low & 0xFFFF) | (high << 16)


def low_of(words):
    return ((words << 16) >> 16).astype(f32)


def high_of(words):
    return (words >> 16).astype(f32)


def quantize(values, factor):
    return jnp.clip(jnp.round(values * factor), -32767.0, 32767.0)


def store_codes(out_ref, source_ref, first, peak):
    code, scale = encode(peak)
    factor = LEVELS / scale
    rows = slice(first, first + 128)

    def tile(j):
        return quantize(source_ref[rows, pl.ds(j * 128, 128)], factor)

    def store(j, high):
        words = words_of(tile(j).astype(jnp.int32), high.astype(jnp.int32))
        out_ref[pl.ds(j, 128, stride=16), :] = words

    @pl.loop(0, 5)
    def _(group):
        for t in range(3):
            j = pl.multiple_of(group * 3, 1) + t
            store(j, tile(j + 16))

    last = tile(31)
    lane = lax.broadcasted_iota(jnp.int32, last.shape, 1)
    store(15, jnp.where(lane < CODE_LANE, last, jnp.where(lane == CODE_LANE, code, 0.0)))


def load_scale(in_ref):
    last = high_of(in_ref[pl.ds(15, 128, stride=16), :])
    return jnp.exp(last[:, CODE_LANE : CODE_LANE + 1] * (LN2 / 256.0)) * (1.0 / LEVELS)


def pivot_halves(pivot_ref):
    rows = [pivot_ref[:, owner].reshape(128, 2 * PB) for owner in range(2)]
    both = jnp.concatenate(rows, axis=0)
    return both[:, :PB], both[:, PB:]


def invert_factor(pa, pb, inv_ref, w, after):
    i0 = lax.broadcasted_iota(jnp.int32, (PB, PB), 0)
    i1 = lax.broadcasted_iota(jnp.int32, (PB, PB), 1)
    eye = (i0 == i1).astype(f32)
    w[:, :PB] = mm_nt(pa, pa) * mm_nt(pb, pb) + shift_value * eye
    w[:, PB:] = eye
    nb = 32
    for block in range(PB // nb):
        g = block * nb
        panel = w[g : g + nb, :]
        sub = lax.broadcasted_iota(jnp.int32, (nb, 128), 0)
        for j in range(0, nb, 8):
            cols = [
                jnp.broadcast_to(panel[:, g + j + t : g + j + t + 1], (nb, 128)) for t in range(8)
            ]
            for t in range(8):
                k = j + t
                pivot = jnp.broadcast_to(cols[t][k : k + 1, :], (nb, 128))
                root = lax.rsqrt(pivot)
                root = root * (1.5 - 0.5 * pivot * root * root)
                left = cols[t] * root
                for u in range(t + 1, 8):
                    cols[u] = cols[u] - left * jnp.broadcast_to(
                        left[j + u : j + u + 1, :], (nb, 128)
                    )
                below = jnp.where(sub > k, left, 0.0)
                below = jnp.where(sub == k, 1.0 - root, below)
                wide = jnp.concatenate([below] * 4, axis=1)
                line = jnp.broadcast_to(panel[k : k + 1, :], (nb, 2 * PB))
                scaled = line * jnp.concatenate([root] * 4, axis=1)
                row_k = jnp.concatenate([sub == k] * 4, axis=1)
                panel = jnp.where(row_k, scaled, panel - wide * scaled)
        w[g : g + nb, :] = panel
        if block in after:
            after[block]()
        if g + nb < PB:
            left = panel[:, g + nb : PB] if (g + nb) % 128 == 0 else panel[:, :PB]
            if (g + nb) % 128 == 0:
                update = lax.dot_general(
                    left, panel, (((0,), (0,)), ((), ())), precision=highest, preferred_element_type=f32
                )
                w[g + nb :, :] = w[g + nb :, :] - update
            else:
                update = lax.dot_general(
                    left, panel, (((0,), (0,)), ((), ())), precision=highest, preferred_element_type=f32
                )
                w[g + nb :, :] = w[g + nb :, :] - update[g + nb :, :]
    inv_ref[...] = jnp.where(i0 >= i1, w[:, PB:], 0.0)


def fit(pa, pb, inv, phi, psi, out_ref, work, peak):
    def chunk(at):
        pair = mm_nt(pa, phi[at, :]) * mm_nt(pb, psi[at, :])
        fitted = jnp.dot(inv, pair, precision=highest, preferred_element_type=f32)
        work[:, at] = fitted
        return jnp.abs(fitted)

    peak[...] = jnp.zeros_like(peak)

    @pl.loop(0, 7)
    def _(j):
        fitted = chunk(pl.ds(pl.multiple_of(j * 512, 512), 512))
        best = peak[...]
        for t in range(4):
            best = jnp.maximum(best, fitted[:, t * 128 : t * 128 + 128])
        peak[...] = best

    fitted = chunk(slice(3584, 4000))
    best = peak[...]
    for t in range(3):
        best = jnp.maximum(best, fitted[:, t * 128 : t * 128 + 128])
    best = jnp.max(best, axis=1, keepdims=True)
    best = jnp.maximum(best, jnp.max(fitted[:, 384:], axis=1, keepdims=True))
    for f in range(2):
        store_codes(out_ref.at[f], work, f * 128, best[f * 128 : f * 128 + 128])


def head_kernel(
    own_ref, phi_ref, psi_ref,
    out_ref, pivot_ref, inv_ref, rows_ref, cols_ref,
    phi, psi, w, work, peak, send1, recv1, send2, recv2, send3, recv3,
    send_row, recv_row, send_move, recv_move, send_col, recv_col, local,
):
    r = lax.axis_index("row")
    c = lax.axis_index("col")
    half = r // 2
    core = lax.rem(r, 2)
    goal_row = 8 * core + c
    goal_col = half
    stays = (goal_row == r) & (goal_col == c)
    source_row = 2 * c + r // 8
    source_col = lax.rem(r, 8)

    def at(row, col):
        return {"row": row, "col": col}

    def remote(source, target, send, recv, device):
        return pltpu.make_async_remote_copy(
            source, target, send, recv, device_id=device, device_id_type=MESH
        )

    loads = [
        pltpu.make_async_copy(phi_ref, phi, local.at[0]),
        pltpu.make_async_copy(psi_ref, psi, local.at[1]),
    ]
    for load in loads:
        load.start()

    barrier = pltpu.get_barrier_semaphore()
    for d in range(1, COLS):
        pl.semaphore_signal(
            barrier, inc=1, device_id=at(r, lax.rem(c + d, COLS)), device_id_type=MESH
        )
    for d in range(1, ROWS):
        pl.semaphore_signal(
            barrier, inc=1, device_id=at(lax.rem(r + d, ROWS), c), device_id_type=MESH
        )

    @pl.when(jnp.logical_not(stays))
    def _():
        for device in (at(goal_row, goal_col), at(source_row, source_col)):
            pl.semaphore_signal(barrier, inc=1, device_id=device, device_id_type=MESH)
        pl.semaphore_wait(barrier, COLS + ROWS)

    @pl.when(stays)
    def _():
        pl.semaphore_wait(barrier, COLS + ROWS - 2)

    x = r // 4
    zl = lax.rem(half, 2)
    y = c // 2
    zh = lax.rem(c, 2)
    mate_col = y * 2 + 1 - zh
    mate_half = x * 2 + 1 - zl
    mate_row = mate_half * 2 + core

    keep_rows = pltpu.make_async_copy(own_ref, rows_ref.at[c], local.at[3])
    goal_half = goal_row // 2
    keep_move = pltpu.make_async_copy(own_ref, cols_ref.at[goal_half], local.at[4])
    move = remote(own_ref, cols_ref.at[goal_half], send_move, recv_move, at(goal_row, goal_col))

    def rows_mate(block):
        return remote(
            own_ref, rows_ref.at[block], send_row.at[0], recv_row.at[0], at(r, mate_col)
        )

    def rows_pair(pair, d, device):
        blocks = rows_ref.at[pl.ds(pair * 2, 2)]
        return remote(blocks, blocks, send_row.at[d], recv_row.at[d], at(r, device * 2 + zh))

    def cols_block(block, send, recv, row):
        return remote(cols_ref.at[block], cols_ref.at[block], send, recv, at(row, c))

    def ahead(v, d):
        return lax.rem(v + d, 4)

    def cols_x(v, d, i, row):
        n = 1 + 2 * (d - 1) + i
        block = v * 2 + (zl if i == 0 else 1 - zl)
        return cols_block(block, send_col.at[n], recv_col.at[n], row)

    keep_rows.start()
    rows_mate(c).start()

    @pl.when(jnp.logical_not(stays))
    def _():
        move.start()

    @pl.when(stays)
    def _():
        keep_move.start()

    def scatter(owner, j):
        return remote(
            own_ref.at[pl.ds(pl.multiple_of(j * 16, 16), 16)],
            pivot_ref.at[j, owner],
            send1.at[j],
            recv1.at[owner],
            at(0, j),
        )

    for owner in range(2):

        @pl.when((r == 0) & (c == owner))
        def _():
            keep = pltpu.make_async_copy(
                own_ref.at[pl.ds(owner * 16, 16)], pivot_ref.at[owner, owner], local.at[2]
            )
            keep.start()
            for d in range(1, COLS):
                scatter(owner, (owner + d) % COLS).start()
            keep.wait()

        @pl.when((r == 0) & (c != owner))
        def _():
            scatter(owner, c).wait_recv()

    def down(d):
        return remote(pivot_ref.at[c], pivot_ref.at[c], send2.at[d], recv2, at(d, c))

    @pl.when(r == 0)
    def _():
        for d in range(1, ROWS):
            down(d).start()

    @pl.when(r != 0)
    def _():
        down(1).wait_recv()

    def across(d):
        return remote(
            pivot_ref.at[c], pivot_ref.at[c], send3.at[d], recv3.at[d], at(r, lax.rem(c + d, COLS))
        )

    for d in range(1, COLS):
        across(d).start()
    for d in range(1, COLS):
        source = lax.rem(c + COLS - d, COLS)
        remote(
            pivot_ref.at[source], pivot_ref.at[source], send3.at[d], recv3.at[d], at(r, source)
        ).wait_recv()

    def step_mates():
        keep_rows.wait()
        rows_mate(mate_col).wait_recv()
        for d in range(1, 4):
            rows_pair(y, d, ahead(y, d)).start()

        @pl.when(jnp.logical_not(stays))
        def _():
            remote(
                own_ref, cols_ref.at[half], send_move, recv_move, at(source_row, source_col)
            ).wait_recv()

        @pl.when(stays)
        def _():
            keep_move.wait()

        cols_block(half, send_col.at[0], recv_col.at[0], mate_row).start()

    def step_x():
        cols_block(mate_half, send_col.at[0], recv_col.at[0], mate_row).wait_recv()
        for i in range(2):
            for d in range(1, 4):
                cols_x(x, d, i, ahead(x, d) * 4 + zl * 2 + core).start()

    step_mates()
    pa, pb = pivot_halves(pivot_ref)
    invert_factor(pa, pb, inv_ref, w, {2: step_x})
    for load in loads:
        load.wait()
    fit(pa, pb, inv_ref[...], phi, psi, out_ref, work, peak)

    for d in range(1, 4):
        source = ahead(y, 4 - d)
        rows_pair(source, d, source).wait_recv()
    for d in range(1, 4):
        source = ahead(x, 4 - d)
        for i in range(2):
            cols_x(source, d, i, source * 4 + zl * 2 + core).wait_recv()

    @pl.when(jnp.logical_not(stays))
    def _():
        move.wait_send()

    for d in range(1, COLS):
        across(d).wait_send()
    rows_mate(c).wait_send()
    cols_block(half, send_col.at[0], recv_col.at[0], mate_row).wait_send()
    for d in range(1, 4):
        rows_pair(y, d, ahead(y, d)).wait_send()
        for i in range(2):
            cols_x(x, d, i, ahead(x, d) * 4 + zl * 2 + core).wait_send()

    @pl.when(r == 0)
    def _():
        for d in range(1, ROWS):
            down(d).wait_send()

    for owner in range(2):

        @pl.when((r == 0) & (c == owner))
        def _():
            for d in range(1, COLS):
                scatter(owner, (owner + d) % COLS).wait_send()


def head(own, phi, psi):
    dma = pltpu.SemaphoreType.DMA
    anywhere = pl.BlockSpec(memory_space=pltpu.HBM)
    return pl.pallas_call(
        head_kernel,
        out_shape=(
            jax.ShapeDtypeStruct((2, WORDS, 128), jnp.int32),
            jax.ShapeDtypeStruct((COLS, 2, 16, 2 * PB), bf16),
            jax.ShapeDtypeStruct((PB, PB), f32),
            jax.ShapeDtypeStruct((COLS, 128, 2 * PB), bf16),
            jax.ShapeDtypeStruct((COLS, 128, 2 * PB), bf16),
        ),
        in_specs=[VMEM, anywhere, anywhere],
        out_specs=(VMEM,) * 5,
        scratch_shapes=[
            pltpu.VMEM((CELLS, PB), bf16),
            pltpu.VMEM((CELLS, PB), bf16),
            pltpu.VMEM((PB, 2 * PB), f32),
            pltpu.VMEM((PB, WIDE), f32),
            pltpu.VMEM((PB, 128), f32),
            dma((COLS,)),
            dma((2,)),
            dma((ROWS,)),
            dma,
            dma((COLS,)),
            dma((COLS,)),
            dma((COLS,)),
            dma((COLS,)),
            dma,
            dma,
            dma((COLS,)),
            dma((COLS,)),
            dma((5,)),
        ],
        compiler_params=pltpu.CompilerParams(
            collective_id=1, has_side_effects=True, vmem_limit_bytes=36 << 20
        ),
        name="head",
    )(own, phi, psi)


def fill_factors(factors):
    def signed(index):
        return jnp.where(2 * index < N, index, index - N).astype(f32)

    ky = signed(lax.broadcasted_iota(jnp.int32, (N, 128), 0))
    kz = signed(lax.broadcasted_iota(jnp.int32, (N, 128), 1))
    base = ky * ky + kz * kz

    @pl.loop(0, N)
    def _(kx):
        fx = signed(jnp.full((N, 128), kx, jnp.int32))
        squared = base + fx * fx
        factor = (4.0 / math.pi / (N * N * N)) / jnp.maximum(squared, 1.0)
        at = pl.ds(pl.multiple_of(kx * N, 16), N)
        factors[at, :] = jnp.where(squared > 0.5, factor, 0.0)


def half_convolution(hx, hxt, hy, wz, wzt, factors, got, sent, high, low, planes, lines, flat, peak):
    scale = load_scale(got)

    @pl.loop(0, 4)
    def _(group):
        for t in range(4):
            j = group * 4 + t
            words = got[pl.ds(j, 128, stride=16), :]
            for s, value in enumerate((low_of(words), high_of(words))):
                at = pl.ds(pl.multiple_of((j + 16 * s) * 128, 128), 128)
                high[:, at], low[:, at] = split(value)

    def z_forward(n, start, line):
        at = pl.ds(start, 256)
        first = high[:, at]
        out = mm(jnp.concatenate([first, low[:, at], first], axis=1), wz[n]) * scale
        planes[line] = out[:, :128]
        planes[line + 1] = out[:, 128:]

    @pl.loop(0, 6)
    def _(g):
        for n in range(4):
            z_forward(n, pl.multiple_of(g * 640 + n * 128, 128), g * 8 + n * 2)

    z_forward(0, 3840, 48)

    def mm3(w, data):
        first, second = split(data)
        return mm(w, jnp.concatenate([first, first, second], axis=0))

    def both(value):
        return value[:, :128], value[:, 128:]

    def line_at(y):
        return pl.ds(pl.multiple_of(y * N, 16), N)

    @pl.loop(0, ROWS // 2)
    def _(pair):
        for yy in range(5):
            halves = []
            for s in range(2):
                at = pl.ds(pl.multiple_of((pair * 2 + s) * 8, 8), 8)
                halves.append(
                    jnp.concatenate([planes[x * 5 + yy, at, :] for x in range(10)], axis=0)
                )
            out = both(mm3(hx, jnp.concatenate(halves, axis=1)))
            for s in range(2):
                lines[line_at((pair * 2 + s) * 5 + yy), :] = out[s]

    @pl.loop(0, N // 8)
    def _(group):
        ats = [pl.ds(group * 8 + t, N, stride=N) for t in range(8)]
        datas = [lines[at, :] for at in ats]
        outs = []
        for t in range(0, 8, 2):
            factor = [factors[line_at(group * 8 + t + s), :] for s in range(2)]
            out = mm3(hy, jnp.concatenate(datas[t : t + 2], axis=1))
            outs.extend(both(mm3(hy, out * jnp.concatenate(factor, axis=1))))
        for at, out in zip(ats, outs, strict=True):
            lines[at, :] = out

    @pl.loop(0, ROWS // 2)
    def _(pair):
        for yy in range(5):
            halves = [lines[line_at((pair * 2 + s) * 5 + yy), :] for s in range(2)]
            out = both(mm3(hxt, jnp.concatenate(halves, axis=1)))
            for s in range(2):
                at = pl.ds(pl.multiple_of((pair * 2 + s) * 8, 8), 8)
                for x in range(10):
                    planes[x * 5 + yy, at, :] = out[s][x * 8 : x * 8 + 8]

    def z_backward(n, line):
        first = split(planes[line])
        second = split(planes[line + 1])
        data = jnp.concatenate(
            [first[0], second[0], first[1], second[1], first[0], second[0]], axis=1
        )
        return both(mm_nt(data, wzt[n]))

    peak[...] = jnp.zeros_like(peak)

    @pl.loop(0, 6)
    def _(g):
        start = pl.multiple_of(g * 640, 128)
        best = peak[...]
        before = None
        for n in range(5):
            value = before
            if n < 4:
                out, after = z_backward(n, g * 8 + n * 2)
                value = out if before is None else out + before
                before = after
            flat[:, pl.ds(start + n * 128, 128)] = value
            best = jnp.maximum(best, jnp.abs(value))
        peak[...] = best

    best = peak[...]
    for t, value in enumerate(z_backward(0, 48)):
        flat[:, 3840 + t * 128 : 3968 + t * 128] = value
        best = jnp.maximum(best, jnp.abs(value))
    store_codes(sent, flat, 0, jnp.max(best, axis=1, keepdims=True))


def grams(left, right):
    return mm_nt(left[:, :PB], right[:, :PB]) * mm_nt(left[:, PB:], right[:, PB:])


def shifted(gram, row, column):
    i = row + lax.broadcasted_iota(jnp.int32, gram.shape, 0)
    j = column + lax.broadcasted_iota(jnp.int32, gram.shape, 1)
    return gram + jnp.where(i == j, shift_value, 0.0)


def panels(pivot_ref, inv_ref, rows_ref, cols_ref, panel_ref, left3, right3, r, c):
    pa, pb = pivot_halves(pivot_ref)
    pivots = jnp.concatenate([pa, pb], axis=1)
    inv = inv_ref[...]

    def panel_of(samples, row):
        return lax.dot_general(
            shifted(grams(samples, pivots), row, 0), inv, (((1,), (1,)), ((), ())),
            precision=highest, preferred_element_type=f32,
        )

    @pl.loop(0, 4)
    def _(i):
        at = pl.ds(pl.multiple_of(i * 256, 256), 256)
        panel = panel_of(rows_ref[at, :], r * 1024 + i * 256)
        panel_ref[at, :] = panel
        high, low = split(panel)
        left3[at, :] = jnp.concatenate([high, low, high], axis=1)

    @pl.loop(0, 8)
    def _(i):
        at = pl.ds(pl.multiple_of(i * 256, 256), 256)
        high, low = split(panel_of(cols_ref[i].reshape(256, 2 * PB), c * 2048 + i * 256))
        right3[at, :] = jnp.concatenate([high, high, low], axis=1)


def schur_tiles(rows_ref, cols_ref, schur_ref, left3, right3, tiles, out_sem, r, c):
    def put(i, slot):
        return pltpu.make_async_copy(
            tiles.at[slot], schur_ref.at[pl.ds(pl.multiple_of(i * 128, 128), 128)], out_sem.at[slot]
        )

    @pl.loop(0, 4)
    def _(pair):
        for slot in range(2):
            i = pair * 2 + slot

            @pl.when(pair > 0)
            def _():
                put(i - 2, slot).wait()

            at = pl.ds(pl.multiple_of(i * 128, 128), 128)
            rows = rows_ref[at, :]
            left = left3[at, :]
            for j in range(4):
                cols = slice(j * 512, j * 512 + 512)
                samples = cols_ref[2 * j : 2 * j + 2].reshape(512, 2 * PB)
                gram = shifted(grams(rows, samples), r * 1024 + i * 128, c * 2048 + j * 512)
                tiles[slot, :, cols] = gram - mm_nt(left, right3[cols, :])
            put(i, slot).start()

    for slot in range(2):
        put(6 + slot, slot).wait()


def middle_kernel(
    h_ref, hx_ref, hxt_ref, hy_ref, codes_ref, pivot_ref, inv_ref, rows_ref, cols_ref,
    back_ref, panel_ref, schur_ref,
    got, sent, wz, wzt, high, low, planes, lines, flat, peak, left3, right3, tiles, samples, factors,
    send_there, recv_there, send_back, recv_back, own_sem, out_sem, twin_sem,
):
    r = lax.axis_index("row")
    c = lax.axis_index("col")
    me = r * COLS + c

    def at(i):
        device = lax.rem(me + i, DEVICES)
        return device, {"row": device // COLS, "col": lax.rem(device, COLS)}

    def block(i):
        return pl.ds(pl.multiple_of(i * 16, 16), 16)

    barrier = pltpu.get_barrier_semaphore()

    @pl.loop(1, DEVICES)
    def _(i):
        pl.semaphore_signal(barrier, inc=1, device_id=at(i)[1], device_id_type=MESH)

    pl.semaphore_wait(barrier, DEVICES - 1)

    def send_all(source, target, send, recv, keep):
        pltpu.make_async_copy(source.at[block(me)], target.at[block(me)], keep).start()

        @pl.loop(1, DEVICES)
        def _(i):
            device, where = at(i)
            pltpu.make_async_remote_copy(
                source.at[block(device)],
                target.at[block(me)],
                send,
                recv,
                device_id=where,
                device_id_type=MESH,
            ).start()

    def wait_all(ref, sem):
        most = ref.at[pl.ds(0, WORDS - 16)]
        pltpu.make_async_copy(most, most, sem).wait()

    def wait_own(source, target, keep):
        pltpu.make_async_copy(source.at[block(me)], target.at[block(me)], keep).wait()

    core = lax.rem(r, 2)
    keep_samples = pltpu.make_async_copy(cols_ref, samples.at[:, core], twin_sem.at[0])

    def twin_copy(k):
        return pltpu.make_async_remote_copy(
            cols_ref,
            samples.at[:, k],
            twin_sem.at[1],
            twin_sem.at[2],
            device_id={"row": r + 1 - 2 * core, "col": c},
            device_id_type=MESH,
        )

    for f in range(2):
        send_all(codes_ref.at[f], got.at[f], send_there.at[f], recv_there.at[f], own_sem.at[f])
    keep_samples.start()
    twin_copy(core).start()

    wz[...] = jnp.zeros_like(wz)
    wzt[...] = jnp.zeros_like(wzt)
    for part, which in enumerate((0, 0, 1)):
        h = h_ref[which]
        for n in range(4):
            for s in range(2):
                first = 32 * n + 80 * s
                wz[n, part * 256 + first : part * 256 + first + 80, 128 * s : 128 * s + 128] = h
                lane = part * 256 + 128 * s
                wzt[n, first : first + 80, lane : lane + 128] = h

    fill_factors(factors)
    keep_samples.wait()
    twin_copy(1 - core).wait_recv()
    panels(pivot_ref, inv_ref, rows_ref, samples, panel_ref, left3, right3, r, c)
    matrices = (hx_ref[...], hxt_ref[...], hy_ref[...])
    for f in range(2):
        wait_own(codes_ref.at[f], got.at[f], own_sem.at[f])
        wait_all(got.at[f], recv_there.at[f])
        half_convolution(
            *matrices, wz, wzt, factors, got.at[f], sent.at[f], high, low, planes, lines, flat, peak
        )
        send_all(sent.at[f], back_ref.at[f], send_back.at[f], recv_back.at[f], own_sem.at[2 + f])
    schur_tiles(rows_ref, samples, schur_ref, left3, right3, tiles, out_sem, r, c)
    for f in range(2):
        wait_own(sent.at[f], back_ref.at[f], own_sem.at[2 + f])
        wait_all(back_ref.at[f], recv_back.at[f])
    for f in range(2):
        wait_all(codes_ref.at[f], send_there.at[f])
        wait_all(sent.at[f], send_back.at[f])
    twin_copy(core).wait_send()


def side_by_side(a):
    high, low = split_np(a)
    return jnp.asarray(np.concatenate([high, low, high], axis=1))


def middle(codes, pivots, inverse, rows, cols):
    h = hartley()
    padded = np.zeros((N, 128))
    padded[:, :N] = h
    h_parts = np.stack(split_np(padded))
    hx = h.reshape(N, COLS, 10).transpose(0, 2, 1).reshape(N, N)
    dma = pltpu.SemaphoreType.DMA
    return pl.pallas_call(
        middle_kernel,
        out_shape=(
            jax.ShapeDtypeStruct((2, WORDS, 128), jnp.int32),
            jax.ShapeDtypeStruct((NMU // ROWS, PB), f32),
            jax.ShapeDtypeStruct((NMU // ROWS, NMU // COLS), f32),
        ),
        in_specs=[VMEM] * 9,
        out_specs=(VMEM, VMEM, pl.BlockSpec(memory_space=pl.ANY)),
        scratch_shapes=[
            pltpu.VMEM((2, WORDS, 128), jnp.int32),
            pltpu.VMEM((2, WORDS, 128), jnp.int32),
            pltpu.VMEM((4, 768, 256), bf16),
            pltpu.VMEM((4, 256, 768), bf16),
            pltpu.VMEM((128, WIDE), bf16),
            pltpu.VMEM((128, WIDE), bf16),
            pltpu.VMEM((50, 128, 128), f32),
            pltpu.VMEM((N * N, 128), f32),
            pltpu.VMEM((128, WIDE), f32),
            pltpu.VMEM((128, 128), f32),
            pltpu.VMEM((NMU // ROWS, 768), bf16),
            pltpu.VMEM((NMU // COLS, 768), bf16),
            pltpu.VMEM((2, 128, NMU // COLS), f32),
            pltpu.VMEM((COLS, 2, 128, 2 * PB), bf16),
            pltpu.VMEM((N * N, 128), f32),
            dma((2,)),
            dma((2,)),
            dma((2,)),
            dma((2,)),
            dma((4,)),
            dma((2,)),
            dma((3,)),
        ],
        compiler_params=pltpu.CompilerParams(
            collective_id=2, has_side_effects=True, vmem_limit_bytes=44 << 20
        ),
        name="middle",
    )(
        jnp.asarray(h_parts),
        side_by_side(hx),
        side_by_side(hx.T),
        side_by_side(h),
        codes,
        pivots,
        inverse,
        rows,
        cols,
    )


def decode_kernel(in_ref, schur_ref, panel_ref, out_ref, schur_out, panel_out, held, sems):
    def pieces(source, target, which):
        copies = []
        for i in range(8):
            at = pl.ds(i * 128, 128)
            ends = [ref if ref is held else ref.at[at] for ref in (source, target)]
            ends = [ref.at[i] if ref is held else ref for ref in ends]
            copies.append(pltpu.make_async_copy(*ends, sems.at[which, i]))
        return copies

    loads = pieces(schur_ref, held, 0)
    stores = pieces(held, schur_out, 1)
    panel_store = pltpu.make_async_copy(panel_ref, panel_out, sems.at[2, 0])
    panel_store.start()
    for load in loads:
        load.start()
    for f in range(2):
        words_ref = in_ref.at[f]
        scale = load_scale(words_ref)
        lanes = slice(f * 128, f * 128 + 128)

        def put(tile, value):
            block = (value * scale).T
            at = pl.ds(pl.multiple_of(tile * 128, 128), 128)
            out_ref[at, lanes] = block

        @pl.loop(0, 5)
        def _(group):
            for t in range(3):
                words = words_ref[pl.ds(group * 3 + t, 128, stride=16), :]
                put(group * 3 + t, low_of(words))
                put(group * 3 + t + 16, high_of(words))

        words = words_ref[pl.ds(15, 128, stride=16), :]
        put(15, low_of(words))
        out_ref[3968:4000, lanes] = (high_of(words) * scale).T[:32]
        if f == 0:
            for load, store in zip(loads, stores, strict=True):
                load.wait()
                store.start()
    for store in stores:
        store.wait()
    panel_store.wait()


def decode(codes, schur, panel):
    anywhere = pl.BlockSpec(memory_space=pltpu.HBM)
    return pl.pallas_call(
        decode_kernel,
        out_shape=(
            jax.ShapeDtypeStruct((CELLS, PB), f32),
            jax.ShapeDtypeStruct(schur.shape, f32),
            jax.ShapeDtypeStruct(panel.shape, f32),
        ),
        in_specs=[VMEM, anywhere, VMEM],
        out_specs=(VMEM, anywhere, anywhere),
        scratch_shapes=[
            pltpu.VMEM((8, 128, NMU // COLS), f32),
            pltpu.SemaphoreType.DMA((3, 8)),
        ],
        compiler_params=pltpu.CompilerParams(vmem_limit_bytes=24 << 20),
        name="decode",
    )(codes, schur, panel)


def in_hbm(a):
    return pltpu.with_memory_space_constraint(a, pltpu.HBM)


def on_device(phi, psi, points):
    col_index = lax.axis_index("col")
    row_index = lax.axis_index("row")
    plane_count, line_count, depth_count, orbital_count = phi.shape
    flat_phi = phi.reshape(CELLS, orbital_count)
    flat_psi = psi.reshape(CELLS, orbital_count)
    global_x = points // (N * N)
    global_y = points // N % N
    global_z = points % N
    local_cell = (
        (global_x - col_index * plane_count) * line_count + global_y - row_index * line_count
    ) * N + global_z
    own = jnp.concatenate(
        [jnp.take(flat_phi, local_cell, axis=0), jnp.take(flat_psi, local_cell, axis=0)], axis=1
    )
    codes, pivots, inverse, row_samples, col_samples = head(own, in_hbm(flat_phi), in_hbm(flat_psi))
    row_samples = row_samples.reshape(NMU // ROWS, 2 * PB)
    back, panel, schur = middle(codes, pivots, inverse, row_samples, col_samples)
    potential, schur, panel = decode(back, in_hbm(schur), panel)
    potential = potential.reshape(plane_count, line_count, depth_count, PB)
    return (schur, panel, potential)


def solution(mesh):
    in_specs = (P("col", "row", None, None), P("col", "row", None, None), P(("row", "col")))
    out_specs = (P("row", "col"), P("row", None), P("col", "row", None, None))
    return jax.shard_map(
        on_device, mesh=mesh, in_specs=in_specs, out_specs=out_specs, check_vma=False
    )
```

```python
import math
import random

import jax
import jax.numpy as jnp
import numpy as np
from jax import lax
from jax.experimental import pallas as pl
from jax.experimental.pallas import tpu as pltpu
from jax.sharding import PartitionSpec as P

NMU = 16384
PB = 256
N = 80
ROWS = 16
COLS = 8
CELLS = 4000
WIDE = 4096
DEVICES = 128
WORDS = DEVICES * 16
CODE_LANE = 4000 - 31 * 128
LEVELS = 32766.0
LN2 = math.log(2.0)
shift_value = 4.0
highest = lax.Precision.HIGHEST
MESH = pl.DeviceIdType.MESH
VMEM = pl.BlockSpec(memory_space=pltpu.VMEM)
f32 = jnp.float32
bf16 = jnp.bfloat16


def far_first():
    every = [(a, b, c, k) for a in range(4) for b in range(4) for c in range(4) for k in range(2)]
    every.remove((0, 0, 0, 0))
    random.Random(1).shuffle(every)
    return sorted(every, key=lambda d: -sum(min(v, 4 - v) for v in d[:3]))


def hartley():
    angle = (np.outer(np.arange(N), np.arange(N)) % N) * (2.0 * np.pi / N)
    return np.cos(angle) + np.sin(angle)


def split_np(a):
    high = a.astype(np.float32).astype(jnp.bfloat16)
    low = (a - high.astype(np.float64)).astype(np.float32).astype(jnp.bfloat16)
    return high, low


def split(a):
    high = a.astype(bf16)
    return high, (a - high.astype(f32)).astype(bf16)


def mm(a, b):
    return jnp.dot(a, b, preferred_element_type=f32)


def mm_nt(a, b):
    return lax.dot_general(a, b, (((1,), (1,)), ((), ())), preferred_element_type=f32)


def encode(peak):
    code = jnp.ceil(jnp.log(jnp.maximum(peak, 1e-30)) * (256.0 / LN2))
    return code, jnp.exp(code * (LN2 / 256.0))


def words_of(low, high):
    return (low & 0xFFFF) | (high << 16)


def low_of(words):
    return ((words << 16) >> 16).astype(f32)


def high_of(words):
    return (words >> 16).astype(f32)


def quantize(values, factor):
    return jnp.clip(jnp.round(values * factor), -32767.0, 32767.0)


def store_codes(out_ref, source_ref, first, peak):
    code, scale = encode(peak)
    factor = LEVELS / scale
    rows = slice(first, first + 128)

    def tile(j):
        return quantize(source_ref[rows, pl.ds(j * 128, 128)], factor)

    def store(j, high):
        words = words_of(tile(j).astype(jnp.int32), high.astype(jnp.int32))
        out_ref[pl.ds(j, 128, stride=16), :] = words

    @pl.loop(0, 5)
    def _(group):
        for t in range(3):
            j = pl.multiple_of(group * 3, 1) + t
            store(j, tile(j + 16))

    last = tile(31)
    lane = lax.broadcasted_iota(jnp.int32, last.shape, 1)
    store(15, jnp.where(lane < CODE_LANE, last, jnp.where(lane == CODE_LANE, code, 0.0)))


def load_scale(in_ref):
    last = high_of(in_ref[pl.ds(15, 128, stride=16), :])
    return jnp.exp(last[:, CODE_LANE : CODE_LANE + 1] * (LN2 / 256.0)) * (1.0 / LEVELS)


def pivot_halves(pivot_ref):
    rows = [pivot_ref[:, owner].reshape(128, 2 * PB) for owner in range(2)]
    both = jnp.concatenate(rows, axis=0)
    return both[:, :PB], both[:, PB:]


def invert_factor(pa, pb, inv_ref, w, after):
    i0 = lax.broadcasted_iota(jnp.int32, (PB, PB), 0)
    i1 = lax.broadcasted_iota(jnp.int32, (PB, PB), 1)
    eye = (i0 == i1).astype(f32)
    w[:, :PB] = mm_nt(pa, pa) * mm_nt(pb, pb) + shift_value * eye
    w[:, PB:] = eye
    nb = 32
    for block in range(PB // nb):
        g = block * nb
        panel = w[g : g + nb, :]
        sub = lax.broadcasted_iota(jnp.int32, (nb, 128), 0)
        for j in range(0, nb, 8):
            cols = [
                jnp.broadcast_to(panel[:, g + j + t : g + j + t + 1], (nb, 128)) for t in range(8)
            ]
            for t in range(8):
                k = j + t
                pivot = jnp.broadcast_to(cols[t][k : k + 1, :], (nb, 128))
                root = lax.rsqrt(pivot)
                root = root * (1.5 - 0.5 * pivot * root * root)
                left = cols[t] * root
                for u in range(t + 1, 8):
                    cols[u] = cols[u] - left * jnp.broadcast_to(
                        left[j + u : j + u + 1, :], (nb, 128)
                    )
                below = jnp.where(sub > k, left, 0.0)
                below = jnp.where(sub == k, 1.0 - root, below)
                wide = jnp.concatenate([below] * 4, axis=1)
                line = jnp.broadcast_to(panel[k : k + 1, :], (nb, 2 * PB))
                scaled = line * jnp.concatenate([root] * 4, axis=1)
                row_k = jnp.concatenate([sub == k] * 4, axis=1)
                panel = jnp.where(row_k, scaled, panel - wide * scaled)
        w[g : g + nb, :] = panel
        if block in after:
            after[block]()
        if g + nb < PB:
            left = panel[:, g + nb : PB] if (g + nb) % 128 == 0 else panel[:, :PB]
            if (g + nb) % 128 == 0:
                update = lax.dot_general(
                    left, panel, (((0,), (0,)), ((), ())), precision=highest, preferred_element_type=f32
                )
                w[g + nb :, :] = w[g + nb :, :] - update
            else:
                update = lax.dot_general(
                    left, panel, (((0,), (0,)), ((), ())), precision=highest, preferred_element_type=f32
                )
                w[g + nb :, :] = w[g + nb :, :] - update[g + nb :, :]
    inv_ref[...] = jnp.where(i0 >= i1, w[:, PB:], 0.0)


def fit(pa, pb, inv, phi, psi, out_ref, work, peak):
    def chunk(at):
        pair = mm_nt(pa, phi[at, :]) * mm_nt(pb, psi[at, :])
        fitted = jnp.dot(inv, pair, precision=highest, preferred_element_type=f32)
        work[:, at] = fitted
        return jnp.abs(fitted)

    peak[...] = jnp.zeros_like(peak)

    @pl.loop(0, 7)
    def _(j):
        fitted = chunk(pl.ds(pl.multiple_of(j * 512, 512), 512))
        best = peak[...]
        for t in range(4):
            best = jnp.maximum(best, fitted[:, t * 128 : t * 128 + 128])
        peak[...] = best

    fitted = chunk(slice(3584, 4000))
    best = peak[...]
    for t in range(3):
        best = jnp.maximum(best, fitted[:, t * 128 : t * 128 + 128])
    best = jnp.max(best, axis=1, keepdims=True)
    best = jnp.maximum(best, jnp.max(fitted[:, 384:], axis=1, keepdims=True))
    for f in range(2):
        store_codes(out_ref.at[f], work, f * 128, best[f * 128 : f * 128 + 128])


def head_kernel(
    own_ref, phi_ref, psi_ref,
    out_ref, pivot_ref, inv_ref, rows_ref, cols_ref,
    phi, psi, w, work, peak, send1, recv1, send2, recv2, send3, recv3,
    send_row, recv_row, send_move, recv_move, send_col, recv_col, local,
):
    r = lax.axis_index("row")
    c = lax.axis_index("col")
    half = r // 2
    core = lax.rem(r, 2)
    goal_row = 8 * core + c
    goal_col = half
    stays = (goal_row == r) & (goal_col == c)
    source_row = 2 * c + r // 8
    source_col = lax.rem(r, 8)

    def at(row, col):
        return {"row": row, "col": col}

    def remote(source, target, send, recv, device):
        return pltpu.make_async_remote_copy(
            source, target, send, recv, device_id=device, device_id_type=MESH
        )

    loads = [
        pltpu.make_async_copy(phi_ref, phi, local.at[0]),
        pltpu.make_async_copy(psi_ref, psi, local.at[1]),
    ]
    for load in loads:
        load.start()

    barrier = pltpu.get_barrier_semaphore()
    for d in range(1, COLS):
        pl.semaphore_signal(
            barrier, inc=1, device_id=at(r, lax.rem(c + d, COLS)), device_id_type=MESH
        )
    for d in range(1, ROWS):
        pl.semaphore_signal(
            barrier, inc=1, device_id=at(lax.rem(r + d, ROWS), c), device_id_type=MESH
        )

    @pl.when(jnp.logical_not(stays))
    def _():
        for device in (at(goal_row, goal_col), at(source_row, source_col)):
            pl.semaphore_signal(barrier, inc=1, device_id=device, device_id_type=MESH)
        pl.semaphore_wait(barrier, COLS + ROWS)

    @pl.when(stays)
    def _():
        pl.semaphore_wait(barrier, COLS + ROWS - 2)

    x = r // 4
    zl = lax.rem(half, 2)
    y = c // 2
    zh = lax.rem(c, 2)
    mate_col = y * 2 + 1 - zh
    mate_half = x * 2 + 1 - zl
    mate_row = mate_half * 2 + core

    keep_rows = pltpu.make_async_copy(own_ref, rows_ref.at[c], local.at[3])
    goal_half = goal_row // 2
    keep_move = pltpu.make_async_copy(own_ref, cols_ref.at[goal_half], local.at[4])
    move = remote(own_ref, cols_ref.at[goal_half], send_move, recv_move, at(goal_row, goal_col))

    def rows_mate(block):
        return remote(
            own_ref, rows_ref.at[block], send_row.at[0], recv_row.at[0], at(r, mate_col)
        )

    def rows_pair(pair, d, device):
        blocks = rows_ref.at[pl.ds(pair * 2, 2)]
        return remote(blocks, blocks, send_row.at[d], recv_row.at[d], at(r, device * 2 + zh))

    def cols_block(block, send, recv, row):
        return remote(cols_ref.at[block], cols_ref.at[block], send, recv, at(row, c))

    def ahead(v, d):
        return lax.rem(v + d, 4)

    def cols_x(v, d, i, row):
        n = 1 + 2 * (d - 1) + i
        block = v * 2 + (zl if i == 0 else 1 - zl)
        return cols_block(block, send_col.at[n], recv_col.at[n], row)

    keep_rows.start()
    rows_mate(c).start()

    @pl.when(jnp.logical_not(stays))
    def _():
        move.start()

    @pl.when(stays)
    def _():
        keep_move.start()

    def scatter(owner, j):
        return remote(
            own_ref.at[pl.ds(pl.multiple_of(j * 16, 16), 16)],
            pivot_ref.at[j, owner],
            send1.at[j],
            recv1.at[owner],
            at(0, j),
        )

    for owner in range(2):

        @pl.when((r == 0) & (c == owner))
        def _():
            keep = pltpu.make_async_copy(
                own_ref.at[pl.ds(owner * 16, 16)], pivot_ref.at[owner, owner], local.at[2]
            )
            keep.start()
            for d in range(1, COLS):
                scatter(owner, (owner + d) % COLS).start()
            keep.wait()

        @pl.when((r == 0) & (c != owner))
        def _():
            scatter(owner, c).wait_recv()

    def down(d):
        return remote(pivot_ref.at[c], pivot_ref.at[c], send2.at[d], recv2, at(d, c))

    @pl.when(r == 0)
    def _():
        for d in range(1, ROWS):
            down(d).start()

    @pl.when(r != 0)
    def _():
        down(1).wait_recv()

    def across(d):
        return remote(
            pivot_ref.at[c], pivot_ref.at[c], send3.at[d], recv3.at[d], at(r, lax.rem(c + d, COLS))
        )

    for d in range(1, COLS):
        across(d).start()
    for d in range(1, COLS):
        source = lax.rem(c + COLS - d, COLS)
        remote(
            pivot_ref.at[source], pivot_ref.at[source], send3.at[d], recv3.at[d], at(r, source)
        ).wait_recv()

    def step_mates():
        keep_rows.wait()
        rows_mate(mate_col).wait_recv()
        for d in range(1, 4):
            rows_pair(y, d, ahead(y, d)).start()

        @pl.when(jnp.logical_not(stays))
        def _():
            remote(
                own_ref, cols_ref.at[half], send_move, recv_move, at(source_row, source_col)
            ).wait_recv()

        @pl.when(stays)
        def _():
            keep_move.wait()

        cols_block(half, send_col.at[0], recv_col.at[0], mate_row).start()

    def step_x():
        cols_block(mate_half, send_col.at[0], recv_col.at[0], mate_row).wait_recv()
        for i in range(2):
            for d in range(1, 4):
                cols_x(x, d, i, ahead(x, d) * 4 + zl * 2 + core).start()

    step_mates()
    pa, pb = pivot_halves(pivot_ref)
    invert_factor(pa, pb, inv_ref, w, {2: step_x})
    for load in loads:
        load.wait()
    fit(pa, pb, inv_ref[...], phi, psi, out_ref, work, peak)

    for d in range(1, 4):
        source = ahead(y, 4 - d)
        rows_pair(source, d, source).wait_recv()
    for d in range(1, 4):
        source = ahead(x, 4 - d)
        for i in range(2):
            cols_x(source, d, i, source * 4 + zl * 2 + core).wait_recv()

    @pl.when(jnp.logical_not(stays))
    def _():
        move.wait_send()

    for d in range(1, COLS):
        across(d).wait_send()
    rows_mate(c).wait_send()
    cols_block(half, send_col.at[0], recv_col.at[0], mate_row).wait_send()
    for d in range(1, 4):
        rows_pair(y, d, ahead(y, d)).wait_send()
        for i in range(2):
            cols_x(x, d, i, ahead(x, d) * 4 + zl * 2 + core).wait_send()

    @pl.when(r == 0)
    def _():
        for d in range(1, ROWS):
            down(d).wait_send()

    for owner in range(2):

        @pl.when((r == 0) & (c == owner))
        def _():
            for d in range(1, COLS):
                scatter(owner, (owner + d) % COLS).wait_send()


def head(own, phi, psi):
    dma = pltpu.SemaphoreType.DMA
    anywhere = pl.BlockSpec(memory_space=pltpu.HBM)
    return pl.pallas_call(
        head_kernel,
        out_shape=(
            jax.ShapeDtypeStruct((2, WORDS, 128), jnp.int32),
            jax.ShapeDtypeStruct((COLS, 2, 16, 2 * PB), bf16),
            jax.ShapeDtypeStruct((PB, PB), f32),
            jax.ShapeDtypeStruct((COLS, 128, 2 * PB), bf16),
            jax.ShapeDtypeStruct((COLS, 128, 2 * PB), bf16),
        ),
        in_specs=[VMEM, anywhere, anywhere],
        out_specs=(VMEM,) * 5,
        scratch_shapes=[
            pltpu.VMEM((CELLS, PB), bf16),
            pltpu.VMEM((CELLS, PB), bf16),
            pltpu.VMEM((PB, 2 * PB), f32),
            pltpu.VMEM((PB, WIDE), f32),
            pltpu.VMEM((PB, 128), f32),
            dma((COLS,)),
            dma((2,)),
            dma((ROWS,)),
            dma,
            dma((COLS,)),
            dma((COLS,)),
            dma((COLS,)),
            dma((COLS,)),
            dma,
            dma,
            dma((COLS,)),
            dma((COLS,)),
            dma((5,)),
        ],
        compiler_params=pltpu.CompilerParams(
            collective_id=1, has_side_effects=True, vmem_limit_bytes=36 << 20
        ),
        name="head",
    )(own, phi, psi)


def fill_factors(factors):
    def signed(index):
        return jnp.where(2 * index < N, index, index - N).astype(f32)

    ky = signed(lax.broadcasted_iota(jnp.int32, (N, 128), 0))
    kz = signed(lax.broadcasted_iota(jnp.int32, (N, 128), 1))
    base = ky * ky + kz * kz

    @pl.loop(0, N)
    def _(kx):
        fx = signed(jnp.full((N, 128), kx, jnp.int32))
        squared = base + fx * fx
        factor = (4.0 / math.pi / (N * N * N)) / jnp.maximum(squared, 1.0)
        at = pl.ds(pl.multiple_of(kx * N, 16), N)
        factors[at, :] = jnp.where(squared > 0.5, factor, 0.0)


def half_convolution(hx, hxt, hy, wz, wzt, factors, got, sent, high, low, planes, lines, flat, peak):
    scale = load_scale(got)

    @pl.loop(0, 4)
    def _(group):
        for t in range(4):
            j = group * 4 + t
            words = got[pl.ds(j, 128, stride=16), :]
            for s, value in enumerate((low_of(words), high_of(words))):
                at = pl.ds(pl.multiple_of((j + 16 * s) * 128, 128), 128)
                high[:, at], low[:, at] = split(value)

    def z_forward(n, start, line):
        at = pl.ds(start, 256)
        first = high[:, at]
        out = mm(jnp.concatenate([first, low[:, at], first], axis=1), wz[n]) * scale
        planes[line] = out[:, :128]
        planes[line + 1] = out[:, 128:]

    @pl.loop(0, 6)
    def _(g):
        for n in range(4):
            z_forward(n, pl.multiple_of(g * 640 + n * 128, 128), g * 8 + n * 2)

    z_forward(0, 3840, 48)

    def mm3(w, data):
        first, second = split(data)
        return mm(w, jnp.concatenate([first, first, second], axis=0))

    def both(value):
        return value[:, :128], value[:, 128:]

    def line_at(y):
        return pl.ds(pl.multiple_of(y * N, 16), N)

    @pl.loop(0, ROWS // 2)
    def _(pair):
        for yy in range(5):
            halves = []
            for s in range(2):
                at = pl.ds(pl.multiple_of((pair * 2 + s) * 8, 8), 8)
                halves.append(
                    jnp.concatenate([planes[x * 5 + yy, at, :] for x in range(10)], axis=0)
                )
            out = both(mm3(hx, jnp.concatenate(halves, axis=1)))
            for s in range(2):
                lines[line_at((pair * 2 + s) * 5 + yy), :] = out[s]

    @pl.loop(0, N // 8)
    def _(group):
        ats = [pl.ds(group * 8 + t, N, stride=N) for t in range(8)]
        datas = [lines[at, :] for at in ats]
        outs = []
        for t in range(0, 8, 2):
            factor = [factors[line_at(group * 8 + t + s), :] for s in range(2)]
            out = mm3(hy, jnp.concatenate(datas[t : t + 2], axis=1))
            outs.extend(both(mm3(hy, out * jnp.concatenate(factor, axis=1))))
        for at, out in zip(ats, outs, strict=True):
            lines[at, :] = out

    @pl.loop(0, ROWS // 2)
    def _(pair):
        for yy in range(5):
            halves = [lines[line_at((pair * 2 + s) * 5 + yy), :] for s in range(2)]
            out = both(mm3(hxt, jnp.concatenate(halves, axis=1)))
            for s in range(2):
                at = pl.ds(pl.multiple_of((pair * 2 + s) * 8, 8), 8)
                for x in range(10):
                    planes[x * 5 + yy, at, :] = out[s][x * 8 : x * 8 + 8]

    def z_backward(n, line):
        first = split(planes[line])
        second = split(planes[line + 1])
        data = jnp.concatenate(
            [first[0], second[0], first[1], second[1], first[0], second[0]], axis=1
        )
        return both(mm_nt(data, wzt[n]))

    peak[...] = jnp.zeros_like(peak)

    @pl.loop(0, 6)
    def _(g):
        start = pl.multiple_of(g * 640, 128)
        best = peak[...]
        before = None
        for n in range(5):
            value = before
            if n < 4:
                out, after = z_backward(n, g * 8 + n * 2)
                value = out if before is None else out + before
                before = after
            flat[:, pl.ds(start + n * 128, 128)] = value
            best = jnp.maximum(best, jnp.abs(value))
        peak[...] = best

    best = peak[...]
    for t, value in enumerate(z_backward(0, 48)):
        flat[:, 3840 + t * 128 : 3968 + t * 128] = value
        best = jnp.maximum(best, jnp.abs(value))
    store_codes(sent, flat, 0, jnp.max(best, axis=1, keepdims=True))


def grams(left, right):
    return mm_nt(left[:, :PB], right[:, :PB]) * mm_nt(left[:, PB:], right[:, PB:])


def shifted(gram, row, column):
    i = row + lax.broadcasted_iota(jnp.int32, gram.shape, 0)
    j = column + lax.broadcasted_iota(jnp.int32, gram.shape, 1)
    return gram + jnp.where(i == j, shift_value, 0.0)


def panels(pivot_ref, inv_ref, rows_ref, cols_ref, panel_ref, left3, right3, r, c):
    pa, pb = pivot_halves(pivot_ref)
    pivots = jnp.concatenate([pa, pb], axis=1)
    inv = inv_ref[...]

    def panel_of(samples, row):
        return lax.dot_general(
            shifted(grams(samples, pivots), row, 0), inv, (((1,), (1,)), ((), ())),
            precision=highest, preferred_element_type=f32,
        )

    @pl.loop(0, 4)
    def _(i):
        at = pl.ds(pl.multiple_of(i * 256, 256), 256)
        panel = panel_of(rows_ref[at, :], r * 1024 + i * 256)
        panel_ref[at, :] = panel
        high, low = split(panel)
        left3[at, :] = jnp.concatenate([high, low, high], axis=1)

    @pl.loop(0, 8)
    def _(i):
        at = pl.ds(pl.multiple_of(i * 256, 256), 256)
        high, low = split(panel_of(cols_ref[i].reshape(256, 2 * PB), c * 2048 + i * 256))
        right3[at, :] = jnp.concatenate([high, high, low], axis=1)


def schur_tiles(rows_ref, cols_ref, schur_ref, left3, right3, tiles, out_sem, r, c):
    def put(i, slot):
        return pltpu.make_async_copy(
            tiles.at[slot], schur_ref.at[pl.ds(pl.multiple_of(i * 128, 128), 128)], out_sem.at[slot]
        )

    @pl.loop(0, 4)
    def _(pair):
        for slot in range(2):
            i = pair * 2 + slot

            @pl.when(pair > 0)
            def _():
                put(i - 2, slot).wait()

            at = pl.ds(pl.multiple_of(i * 128, 128), 128)
            rows = rows_ref[at, :]
            left = left3[at, :]
            for j in range(4):
                cols = slice(j * 512, j * 512 + 512)
                samples = cols_ref[2 * j : 2 * j + 2].reshape(512, 2 * PB)
                gram = shifted(grams(rows, samples), r * 1024 + i * 128, c * 2048 + j * 512)
                tiles[slot, :, cols] = gram - mm_nt(left, right3[cols, :])
            put(i, slot).start()

    for slot in range(2):
        put(6 + slot, slot).wait()


def middle_kernel(
    h_ref, hx_ref, hxt_ref, hy_ref, codes_ref, pivot_ref, inv_ref, rows_ref, cols_ref,
    back_ref, panel_ref, schur_ref,
    got, sent, wz, wzt, high, low, planes, lines, flat, peak, left3, right3, tiles, samples, factors,
    send_there, recv_there, send_back, recv_back, own_sem, out_sem, twin_sem,
):
    r = lax.axis_index("row")
    c = lax.axis_index("col")
    me = r * COLS + c

    def at(i):
        device = lax.rem(me + i, DEVICES)
        return device, {"row": device // COLS, "col": lax.rem(device, COLS)}

    def block(i):
        return pl.ds(pl.multiple_of(i * 16, 16), 16)

    barrier = pltpu.get_barrier_semaphore()

    @pl.loop(1, DEVICES)
    def _(i):
        pl.semaphore_signal(barrier, inc=1, device_id=at(i)[1], device_id_type=MESH)

    pl.semaphore_wait(barrier, DEVICES - 1)

    x, z, y = r // 4, lax.rem(c, 2) * 2 + lax.rem(r // 2, 2), c // 2
    xs = [lax.rem(x + d, 4) * 4 for d in range(4)]
    ys = [lax.rem(y + d, 4) * 2 for d in range(4)]
    zs = [lax.rem(z + d, 4) for d in range(4)]
    z_rows = [lax.rem(v, 2) * 2 for v in zs]
    z_cols = [v // 2 for v in zs]
    ks = [lax.rem(r + d, 2) for d in range(2)]
    z_cores = [[v + k for k in ks] for v in z_rows]
    cols = [[v + w for w in z_cols] for v in ys]

    def send_all(source, target, send, recv, keep):
        pltpu.make_async_copy(source.at[block(me)], target.at[block(me)], keep).start()
        for dx, dy, dz, dk in far_first():
            row, col = xs[dx] + z_cores[dz][dk], cols[dy][dz]
            pltpu.make_async_remote_copy(
                source.at[block(row * COLS + col)],
                target.at[block(me)],
                send,
                recv,
                device_id={"row": row, "col": col},
                device_id_type=MESH,
            ).start()

    def wait_all(ref, sem):
        most = ref.at[pl.ds(0, WORDS - 16)]
        pltpu.make_async_copy(most, most, sem).wait()

    def wait_own(source, target, keep):
        pltpu.make_async_copy(source.at[block(me)], target.at[block(me)], keep).wait()

    core = lax.rem(r, 2)
    keep_samples = pltpu.make_async_copy(cols_ref, samples.at[:, core], twin_sem.at[0])

    def twin_copy(k):
        return pltpu.make_async_remote_copy(
            cols_ref,
            samples.at[:, k],
            twin_sem.at[1],
            twin_sem.at[2],
            device_id={"row": r + 1 - 2 * core, "col": c},
            device_id_type=MESH,
        )

    for f in range(2):
        send_all(codes_ref.at[f], got.at[f], send_there.at[f], recv_there.at[f], own_sem.at[f])
    keep_samples.start()
    twin_copy(core).start()

    wz[...] = jnp.zeros_like(wz)
    wzt[...] = jnp.zeros_like(wzt)
    for part, which in enumerate((0, 0, 1)):
        h = h_ref[which]
        for n in range(4):
            for s in range(2):
                first = 32 * n + 80 * s
                wz[n, part * 256 + first : part * 256 + first + 80, 128 * s : 128 * s + 128] = h
                lane = part * 256 + 128 * s
                wzt[n, first : first + 80, lane : lane + 128] = h

    fill_factors(factors)
    keep_samples.wait()
    twin_copy(1 - core).wait_recv()
    panels(pivot_ref, inv_ref, rows_ref, samples, panel_ref, left3, right3, r, c)
    matrices = (hx_ref[...], hxt_ref[...], hy_ref[...])
    for f in range(2):
        wait_own(codes_ref.at[f], got.at[f], own_sem.at[f])
        wait_all(got.at[f], recv_there.at[f])
        half_convolution(
            *matrices, wz, wzt, factors, got.at[f], sent.at[f], high, low, planes, lines, flat, peak
        )
        send_all(sent.at[f], back_ref.at[f], send_back.at[f], recv_back.at[f], own_sem.at[2 + f])
    schur_tiles(rows_ref, samples, schur_ref, left3, right3, tiles, out_sem, r, c)
    for f in range(2):
        wait_own(sent.at[f], back_ref.at[f], own_sem.at[2 + f])
        wait_all(back_ref.at[f], recv_back.at[f])
    for f in range(2):
        wait_all(codes_ref.at[f], send_there.at[f])
        wait_all(sent.at[f], send_back.at[f])
    twin_copy(core).wait_send()


def side_by_side(a):
    high, low = split_np(a)
    return jnp.asarray(np.concatenate([high, low, high], axis=1))


def middle(codes, pivots, inverse, rows, cols):
    h = hartley()
    padded = np.zeros((N, 128))
    padded[:, :N] = h
    h_parts = np.stack(split_np(padded))
    hx = h.reshape(N, COLS, 10).transpose(0, 2, 1).reshape(N, N)
    dma = pltpu.SemaphoreType.DMA
    return pl.pallas_call(
        middle_kernel,
        out_shape=(
            jax.ShapeDtypeStruct((2, WORDS, 128), jnp.int32),
            jax.ShapeDtypeStruct((NMU // ROWS, PB), f32),
            jax.ShapeDtypeStruct((NMU // ROWS, NMU // COLS), f32),
        ),
        in_specs=[VMEM] * 9,
        out_specs=(VMEM, VMEM, pl.BlockSpec(memory_space=pl.ANY)),
        scratch_shapes=[
            pltpu.VMEM((2, WORDS, 128), jnp.int32),
            pltpu.VMEM((2, WORDS, 128), jnp.int32),
            pltpu.VMEM((4, 768, 256), bf16),
            pltpu.VMEM((4, 256, 768), bf16),
            pltpu.VMEM((128, WIDE), bf16),
            pltpu.VMEM((128, WIDE), bf16),
            pltpu.VMEM((50, 128, 128), f32),
            pltpu.VMEM((N * N, 128), f32),
            pltpu.VMEM((128, WIDE), f32),
            pltpu.VMEM((128, 128), f32),
            pltpu.VMEM((NMU // ROWS, 768), bf16),
            pltpu.VMEM((NMU // COLS, 768), bf16),
            pltpu.VMEM((2, 128, NMU // COLS), f32),
            pltpu.VMEM((COLS, 2, 128, 2 * PB), bf16),
            pltpu.VMEM((N * N, 128), f32),
            dma((2,)),
            dma((2,)),
            dma((2,)),
            dma((2,)),
            dma((4,)),
            dma((2,)),
            dma((3,)),
        ],
        compiler_params=pltpu.CompilerParams(
            collective_id=2, has_side_effects=True, vmem_limit_bytes=44 << 20
        ),
        name="middle",
    )(
        jnp.asarray(h_parts),
        side_by_side(hx),
        side_by_side(hx.T),
        side_by_side(h),
        codes,
        pivots,
        inverse,
        rows,
        cols,
    )


def decode_kernel(
    in_ref, schur_ref, panel_ref, result_ref, schur_out, panel_out, held, out_ref, sems, out_sems
):
    def pieces(source, target, which):
        copies = []
        for i in range(8):
            at = pl.ds(i * 128, 128)
            ends = [ref if ref is held else ref.at[at] for ref in (source, target)]
            ends = [ref.at[i] if ref is held else ref for ref in ends]
            copies.append(pltpu.make_async_copy(*ends, sems.at[which, i]))
        return copies

    loads = pieces(schur_ref, held, 0)
    stores = pieces(held, schur_out, 1)
    panel_store = pltpu.make_async_copy(panel_ref, panel_out, sems.at[2, 0])
    panel_store.start()
    for load in loads:
        load.start()
    scales = [load_scale(in_ref.at[f]) for f in range(2)]
    results = []

    def decoded(j):
        for f in range(2):
            lanes = slice(f * 128, f * 128 + 128)
            words = in_ref[f, pl.ds(j, 128, stride=16), :]
            out_ref[j * 128 : j * 128 + 128, lanes] = (low_of(words) * scales[f]).T
            start = (j + 16) * 128
            rows = min(CELLS - start, 128)
            out_ref[start : start + rows, lanes] = (high_of(words) * scales[f]).T[:rows]

    def put(start, rows):
        at = pl.ds(start, rows)
        copy = pltpu.make_async_copy(
            out_ref.at[at], result_ref.at[at], out_sems.at[len(results)]
        )
        copy.start()
        results.append(copy)

    for group in range(5):
        for t in range(3):
            decoded(group * 3 + t)
        put(group * 384, 384)
        put(2048 + group * 384, 384)
        if group:
            for piece in (group * 2 - 2, group * 2 - 1):
                loads[piece].wait()
                stores[piece].start()
    decoded(15)
    put(1920, 128)
    put(3968, 32)
    for store in stores:
        store.wait()
    for copy in results:
        copy.wait()
    panel_store.wait()


def decode(codes, schur, panel):
    anywhere = pl.BlockSpec(memory_space=pltpu.HBM)
    return pl.pallas_call(
        decode_kernel,
        out_shape=(
            jax.ShapeDtypeStruct((CELLS, PB), f32),
            jax.ShapeDtypeStruct(schur.shape, f32),
            jax.ShapeDtypeStruct(panel.shape, f32),
        ),
        in_specs=[VMEM, anywhere, VMEM],
        out_specs=(anywhere,) * 3,
        scratch_shapes=[
            pltpu.VMEM((8, 128, NMU // COLS), f32),
            pltpu.VMEM((CELLS, PB), f32),
            pltpu.SemaphoreType.DMA((3, 8)),
            pltpu.SemaphoreType.DMA((12,)),
        ],
        compiler_params=pltpu.CompilerParams(vmem_limit_bytes=24 << 20),
        name="decode",
    )(codes, schur, panel)


def in_hbm(a):
    return pltpu.with_memory_space_constraint(a, pltpu.HBM)


def on_device(phi, psi, points):
    col_index = lax.axis_index("col")
    row_index = lax.axis_index("row")
    plane_count, line_count, depth_count, orbital_count = phi.shape
    flat_phi = phi.reshape(CELLS, orbital_count)
    flat_psi = psi.reshape(CELLS, orbital_count)
    global_x = points // (N * N)
    global_y = points // N % N
    global_z = points % N
    local_cell = (
        (global_x - col_index * plane_count) * line_count + global_y - row_index * line_count
    ) * N + global_z
    own = jnp.concatenate(
        [jnp.take(flat_phi, local_cell, axis=0), jnp.take(flat_psi, local_cell, axis=0)], axis=1
    )
    codes, pivots, inverse, row_samples, col_samples = head(own, in_hbm(flat_phi), in_hbm(flat_psi))
    row_samples = row_samples.reshape(NMU // ROWS, 2 * PB)
    back, panel, schur = middle(codes, pivots, inverse, row_samples, col_samples)
    potential, schur, panel = decode(back, in_hbm(schur), panel)
    potential = potential.reshape(plane_count, line_count, depth_count, PB)
    return (schur, panel, potential)


def solution(mesh):
    in_specs = (P("col", "row", None, None), P("col", "row", None, None), P(("row", "col")))
    out_specs = (P("row", "col"), P("row", None), P("col", "row", None, None))
    return jax.shard_map(
        on_device, mesh=mesh, in_specs=in_specs, out_specs=out_specs, check_vma=False
    )
```
